32 devices in a mesh: grp: 2 (over y), frm: 4 (over z), head: 2 (over x), pos: 2 (over core).
Axes of the slice: x: 2, y: 2, z: 4, core: 2. Of those that a mesh axis runs over, the one named last changes fastest.
Arguments:
- queries: float32 [32, 128, 3072], P(('grp', 'frm'), 'pos', 'head'), parts along dimension 0, may hold values from -120 to 120
- key_states: float32 [32, 128, 3072], P(('grp', 'frm'), 'pos', 'head'), parts along dimension 0, may hold values from -4 to 4
- value_states: float32 [32, 128, 3072], P(('grp', 'frm'), 'pos', 'head'), parts along dimension 0, may hold values from -6 to 6
- windows: int32 [24], P('head'), may hold values from 1 to 2, as said below
- strides: int32 [24], P('head'), may hold values from 4 to 8, as said below
- cutoffs: int32 [24], P('head'), may hold values from 1 to 2, as said below
Outputs:
- blended: float32 [32, 128, 3072], P(('grp', 'frm'), 'pos', 'head'), parts along dimension 0
The draws below stay inside these ranges and needn't reach their ends.
There are 2 independent parts, one for each index of `grp`. The reference program is written for one: setup_inputs(seed, part) draws one part's arguments, and reference() takes and returns one part's arrays. A program takes and returns all parts, laid end to end along the dimension named above; an argument that names none is the same for every part. Nothing has to cross between parts.
Inputs may be any that keep to these rules, and one draw needn't show every extreme that they name: `windows`: some head has exactly 2. `strides`: each is 4 or 8, and both occur. `cutoffs`: some head has exactly 2.
All inputs are finite; a program needn't handle non-finite values.
Results may differ from the reference program's by a relative error of at most 0.0003.
Values sent between devices are 32-bit elements; how exact they have to be, the bound alone decides.
No kernel may reach another device: no remote copies, remote signals or barrier semaphores. Data moves between devices by JAX's collectives and lax.ppermute only.
A program may use at most 128 MiB of HBM per device.

```python
import jax
import jax.numpy as jnp
from jax import lax

HEADS = 24
DH = 128
TOK_FRAME = 128
KSTRIDE = 4
FRAMES = 16
WMAX = 2
CMAX = 2


def shared_keys(key):
    split_one = jax.random.fold_in(jax.random.fold_in(key, 7), 0)
    key_values = jnp.clip(jax.random.normal(split_one, (FRAMES, TOK_FRAME, HEADS * DH), jnp.float32), -4.0, 4.0)
    return key_values


def draw_key_states(key, part):
    return shared_keys(key)


def draw_queries(key, part):
    query_key = jax.random.fold_in(key, 13)
    return 2.0 * jnp.clip(jax.random.normal(query_key, (FRAMES, TOK_FRAME, HEADS * DH), jnp.float32), -4.0, 4.0)


def draw_windows(key, part):
    split_one, split_two = jax.random.split(jax.random.fold_in(key, 21))
    drawn_widths = jax.random.randint(split_one, (HEADS,), 1, WMAX + 1)
    chosen = jax.random.randint(split_two, (), 0, HEADS)
    return drawn_widths.at[chosen].set(WMAX).astype(jnp.int32)


def draw_strides(key, part):
    split_one, split_two, split_three = jax.random.split(jax.random.fold_in(key, 31), 3)
    factors = jax.random.randint(split_one, (HEADS,), 1, 3)
    chosen = jax.random.randint(split_two, (), 0, HEADS)
    partner_head = (chosen + jax.random.randint(split_three, (), 1, HEADS)) % HEADS
    factors = factors.at[chosen].set(1).at[partner_head].set(2)
    return (factors * KSTRIDE).astype(jnp.int32)


def draw_cutoffs(key, part):
    split_one, split_two = jax.random.split(jax.random.fold_in(key, 41))
    drawn_cuts = jax.random.randint(split_one, (HEADS,), 1, CMAX + 1)
    chosen = jax.random.randint(split_two, (), 0, HEADS)
    return drawn_cuts.at[chosen].set(CMAX).astype(jnp.int32)


def block_levels(stream_key, dims, cuts, least, top_value):
    level = 1.0
    for axis_at, blocks in cuts:
        draws = jax.random.uniform(jax.random.fold_in(jax.random.fold_in(stream_key, 6), axis_at), (blocks,), jnp.float32, least / len(cuts), top_value / len(cuts))
        level = level * jnp.repeat(jnp.exp(draws), dims[axis_at] // blocks).reshape((-1,) + (1,) * (len(dims) - 1 - axis_at))
    return level


def noise(key, dims, spread, most, shards=(), kind=jnp.bfloat16):
    array = jax.random.normal(key, dims, jnp.float32) * spread
    if len(shards) > 0:
        array = block_levels(key, dims, shards, -0.22, 0.18) * array
    return jnp.clip(array, min=-most, max=most).astype(kind)


def setup_inputs(seed: int = 0, part: int = 0) -> dict:
    arg_keys = jax.random.split(jax.random.key(seed), 7)
    part_keys = jax.random.split(jax.random.fold_in(arg_keys[6], part), 7)
    return {
        "queries": draw_queries(jax.random.fold_in(jax.random.fold_in(arg_keys[6], part), 71), part),
        "key_states": draw_key_states(jax.random.fold_in(jax.random.fold_in(arg_keys[6], part), 71), part),
        "value_states": noise(part_keys[2], (FRAMES, TOK_FRAME, HEADS * DH), 1.0, 6.0, ((0, 4), (1, 2), (2, 2)), jnp.float32),
        "windows": draw_windows(jax.random.fold_in(arg_keys[6], 71), part),
        "strides": draw_strides(jax.random.fold_in(arg_keys[6], 71), part),
        "cutoffs": draw_cutoffs(jax.random.fold_in(arg_keys[6], 71), part),
    }


def masked_attend(query_part, key_part, value_part, allowed, score_scale):
    scores = jnp.einsum('phd,khd->hpk', query_part, key_part, precision=lax.Precision.HIGHEST) * score_scale
    highest = jnp.max(jnp.where(allowed[:, None, :], scores, -1e30), axis=2, keepdims=True)
    weights = jnp.where(allowed[:, None, :], jnp.exp(scores - highest), 0.0)
    row_total = jnp.sum(weights, axis=2, keepdims=True)
    return jnp.einsum('hpk,khd->phd', weights / row_total, value_part, precision=lax.Precision.HIGHEST)


def reference(queries, key_states, value_states, windows, strides, cutoffs):
    score_scale = DH ** -0.5
    query_grid = queries.reshape(FRAMES, TOK_FRAME, HEADS, DH)
    key_grid = key_states.reshape(FRAMES, TOK_FRAME, HEADS, DH)
    value_grid = value_states.reshape(FRAMES, TOK_FRAME, HEADS, DH)
    padding = ((WMAX, WMAX), (0, 0), (0, 0), (0, 0))
    padded_keys = jnp.pad(key_grid, padding)
    padded_values = jnp.pad(value_grid, padding)
    window_span = 2 * WMAX + 1
    key_offsets = jnp.repeat(jnp.arange(window_span, dtype=jnp.int32) - WMAX, TOK_FRAME)
    global_keys = key_grid[::KSTRIDE].reshape(-1, HEADS, DH)
    global_values = value_grid[::KSTRIDE].reshape(-1, HEADS, DH)
    global_frames = jnp.repeat(jnp.arange(0, FRAMES, KSTRIDE, dtype=jnp.int32), TOK_FRAME)
    global_allowed = (global_frames[None, :] % strides[:, None]) == 0

    def per_frame(frame_index):
        query_part = lax.dynamic_index_in_dim(query_grid, frame_index, 0, keepdims=False)
        near_keys = lax.dynamic_slice_in_dim(padded_keys, frame_index, window_span, 0).reshape(window_span * TOK_FRAME, HEADS, DH)
        near_values = lax.dynamic_slice_in_dim(padded_values, frame_index, window_span, 0).reshape(window_span * TOK_FRAME, HEADS, DH)
        near_frames = frame_index + key_offsets
        inside = (near_frames >= 0) & (near_frames < FRAMES)
        local_allowed = inside[None, :] & (jnp.abs(key_offsets)[None, :] <= windows[:, None])
        local_part = masked_attend(query_part, near_keys, near_values, local_allowed, score_scale)
        global_part = masked_attend(query_part, global_keys, global_values, global_allowed, score_scale)
        return local_part, global_part

    local, global_out = lax.map(per_frame, jnp.arange(FRAMES, dtype=jnp.int32))
    difference = global_out - local
    spectrum = jnp.fft.fft(difference, axis=0)
    frequency = jnp.arange(FRAMES, dtype=jnp.int32)
    distance_freq = jnp.minimum(frequency, FRAMES - frequency)
    low_keep = (distance_freq[:, None] <= cutoffs[None, :]).astype(difference.dtype)
    filtered = jnp.real(jnp.fft.ifft(spectrum * low_keep[:, None, :, None], axis=0))
    return (local + filtered).reshape(FRAMES, TOK_FRAME, HEADS * DH)
```

```python
import functools
import math

import jax
import jax.numpy as jnp
import numpy as np
from jax import lax
from jax.experimental import pallas as pl
from jax.experimental.pallas import tpu as pltpu
from jax.sharding import PartitionSpec as P

DH = 128
KSTRIDE = 4
WMAX = 2
MASKED = -1e30


def lowpass_table(frames):
    cutoff = np.arange(frames // 2 + 1)
    freq = np.arange(frames)
    keep = (np.minimum(freq, frames - freq)[None, :] <= cutoff[:, None]).astype(np.float64)
    waves = np.cos(2.0 * np.pi / frames * (np.outer(freq, freq) % frames))
    return (keep @ waves / frames).astype(np.float32)


def pack_kernel(slot, parts, per_part, *refs):
    sources, outs = refs[:3], refs[3 : 3 + parts]
    held, load_sem, store_sem = refs[3 + parts :]
    me = lax.axis_index("frm")
    order = [*range(1, parts), 0]
    loads, stores = {}, {}
    for hop in order:
        owner = lax.rem(me + hop, parts)
        columns = pl.ds(pl.multiple_of((owner * per_part + slot) * DH, DH), DH)
        for at in range(3):
            loads[hop, at] = pltpu.make_async_copy(
                sources[at].at[:, :, columns], held.at[hop, at], load_sem.at[hop, at]
            )
            loads[hop, at].start()
    for hop in order:
        for at in range(3):
            loads[hop, at].wait()
        stores[hop] = pltpu.make_async_copy(held.at[hop], outs[hop], store_sem.at[hop])
        stores[hop].start()
    for hop in order:
        stores[hop].wait()


def pack(slot, parts, queries, key_states, value_states):
    frames_dev, rows, channels = queries.shape
    piece = (3, frames_dev, rows, DH)
    moved = parts * math.prod(piece) * 4
    return pl.pallas_call(
        functools.partial(pack_kernel, slot, parts, channels // DH // parts),
        out_shape=[jax.ShapeDtypeStruct(piece, jnp.float32)] * parts,
        in_specs=[pl.BlockSpec(memory_space=pl.ANY)] * 3,
        out_specs=[pl.BlockSpec(memory_space=pl.ANY)] * parts,
        scratch_shapes=[
            pltpu.VMEM((parts, *piece), jnp.float32),
            pltpu.SemaphoreType.DMA((parts, 3)),
            pltpu.SemaphoreType.DMA((parts,)),
        ],
        cost_estimate=pl.CostEstimate(flops=0, bytes_accessed=2 * moved, transcendentals=0),
        name=f"pack{slot}",
    )(queries, key_states, value_states)


def split(value):
    high = value.astype(jnp.bfloat16)
    return high, (value - high.astype(jnp.float32)).astype(jnp.bfloat16)


def weighted(scores, values):
    highest = jnp.max(scores, axis=1, keepdims=True)
    weights = jnp.exp(scores - highest)
    total = jnp.sum(weights, axis=1, keepdims=True)
    high, low = split(weights)
    wide = jnp.dot(high, values, preferred_element_type=jnp.float32)
    rest = jnp.dot(low, values[:, :DH], preferred_element_type=jnp.float32)
    return (wide[:, :DH] + wide[:, DH:] + rest) / total


def attend_kernel(slot, parts, per_part, *refs):
    windows, strides, cutoffs, table = refs[:4]
    mine, theirs = refs[4 : 4 + parts], refs[4 + parts : 4 + 2 * parts]
    outs = refs[4 + 2 * parts : 4 + 3 * parts]
    (q_in, k_in, v_in, q_cat, k_cat, v_cat, kg_cat, vg_cat, local, diff, load_sem, store_sem) = refs[
        4 + 3 * parts :
    ]
    frames, rows, _ = q_in.shape
    tokens = k_in.shape[1]
    frames_dev = frames // parts
    me = lax.axis_index("frm")
    head = me * per_part + slot
    window, stride, cutoff = windows[head], strides[head], cutoffs[head]

    loads = []
    for hop in range(parts):
        owner = lax.rem(me + parts - hop, parts)
        span = pl.ds(owner * frames_dev, frames_dev)
        near, far = pl.ds(0, rows), pl.ds(rows, rows)
        for at, (source, target) in enumerate(
            (
                (mine[hop].at[0], q_in.at[span]),
                (mine[hop].at[1], k_in.at[span, near]),
                (mine[hop].at[2], v_in.at[span, near]),
                (theirs[hop].at[1], k_in.at[span, far]),
                (theirs[hop].at[2], v_in.at[span, far]),
            )
        ):
            copy = pltpu.make_async_copy(source, target, load_sem.at[hop, at])
            copy.start()
            loads.append(copy)
    for copy in loads:
        copy.wait()

    score_scale = DH ** (-0.5)

    def prepare(frame, carry):
        q_at = pl.ds(pl.multiple_of(frame * rows, rows), rows)
        k_at = pl.ds(pl.multiple_of(frame * tokens, tokens), tokens)
        high, low = split(q_in[frame] * score_scale)
        q_cat[q_at, 0:DH] = high
        q_cat[q_at, DH : 2 * DH] = low
        q_cat[q_at, 2 * DH : 3 * DH] = high
        k_high, k_low = split(k_in[frame])
        k_cat[k_at, 0:DH] = k_high
        k_cat[k_at, DH : 2 * DH] = k_high
        k_cat[k_at, 2 * DH : 3 * DH] = k_low
        v_high, v_low = split(v_in[frame])
        v_cat[k_at, 0:DH] = v_high
        v_cat[k_at, DH : 2 * DH] = v_low
        return carry

    lax.fori_loop(0, frames, prepare, 0)
    key_frames = frames // KSTRIDE
    for at in range(key_frames):
        source = pl.ds(at * KSTRIDE * tokens, tokens)
        target = pl.ds(at * tokens, tokens)
        kg_cat[target, :] = k_cat[source, :]
        vg_cat[target, :] = v_cat[source, :]

    def scores_of(query_rows, key_rows):
        return lax.dot_general(
            query_rows, key_rows, (((1,), (1,)), ((), ())), preferred_element_type=jnp.float32
        )

    pair = 2
    reach = min(2 * WMAX + pair, frames)
    pair_rows = pair * rows
    key_frame = lax.broadcasted_iota(jnp.int32, (1, key_frames * tokens), 1) // tokens * KSTRIDE
    global_bias = jnp.where(lax.rem(key_frame, stride) == 0, 0.0, MASKED)

    def per_pair(step, carry):
        first = step * pair
        start = jnp.clip(first - WMAX, 0, frames - reach)
        q_part = q_cat[pl.ds(pl.multiple_of(first * rows, pair_rows), pair_rows), :]
        k_at = pl.ds(pl.multiple_of(start * tokens, tokens), reach * tokens)
        near_frame = start + lax.broadcasted_iota(jnp.int32, (pair_rows, reach * tokens), 1) // tokens
        query_frame = first + lax.broadcasted_iota(jnp.int32, (pair_rows, reach * tokens), 0) // rows
        scores = scores_of(q_part, k_cat[k_at, :])
        scores = jnp.where(jnp.abs(near_frame - query_frame) <= window, scores, MASKED)
        local_part = weighted(scores, v_cat[k_at, :])
        global_part = weighted(scores_of(q_part, kg_cat[...]) + global_bias, vg_cat[...])
        difference = global_part - local_part
        for at in range(pair):
            local[first + at] = local_part[at * rows : (at + 1) * rows]
            diff[first + at] = difference[at * rows : (at + 1) * rows]
        return carry

    lax.fori_loop(0, frames // pair, per_pair, 0)

    kept = jnp.clip(cutoff, 0, frames // 2)

    def blend(frame, carry):
        total = local[frame]
        for other in range(frames):
            total += table[kept, lax.rem(frame + frames - other, frames)] * diff[other]
        q_in[frame] = total
        return carry

    lax.fori_loop(0, frames, blend, 0)
    stores = []
    for hop in range(parts):
        owner = lax.rem(me + hop, parts)
        stores.append(
            pltpu.make_async_copy(
                q_in.at[pl.ds(owner * frames_dev, frames_dev)], outs[hop], store_sem.at[hop]
            )
        )
        stores[-1].start()
    for copy in stores:
        copy.wait()


def attend_head(slot, parts, scalars, table, mine, theirs):
    _, frames_dev, rows, _ = mine[0].shape
    frames, tokens = frames_dev * parts, 2 * rows
    per_part = scalars[0].shape[0] // parts
    key_frames = frames // KSTRIDE
    flops = 12 * frames * rows * (5 + key_frames) * tokens * DH
    return pl.pallas_call(
        functools.partial(attend_kernel, slot, parts, per_part),
        out_shape=[jax.ShapeDtypeStruct((frames_dev, rows, DH), jnp.float32)] * parts,
        in_specs=[pl.BlockSpec(memory_space=pltpu.SMEM)] * 4
        + [pl.BlockSpec(memory_space=pl.ANY)] * (2 * parts),
        out_specs=[pl.BlockSpec(memory_space=pl.ANY)] * parts,
        scratch_shapes=[
            pltpu.VMEM((frames, rows, DH), jnp.float32),
            pltpu.VMEM((frames, tokens, DH), jnp.float32),
            pltpu.VMEM((frames, tokens, DH), jnp.float32),
            pltpu.VMEM((frames * rows, 3 * DH), jnp.bfloat16),
            pltpu.VMEM((frames * tokens, 3 * DH), jnp.bfloat16),
            pltpu.VMEM((frames * tokens, 2 * DH), jnp.bfloat16),
            pltpu.VMEM((key_frames * tokens, 3 * DH), jnp.bfloat16),
            pltpu.VMEM((key_frames * tokens, 2 * DH), jnp.bfloat16),
            pltpu.VMEM((frames, rows, DH), jnp.float32),
            pltpu.VMEM((frames, rows, DH), jnp.float32),
            pltpu.SemaphoreType.DMA((parts, 5)),
            pltpu.SemaphoreType.DMA((parts,)),
        ],
        cost_estimate=pl.CostEstimate(
            flops=flops,
            bytes_accessed=6 * frames * rows * DH * 4,
            transcendentals=frames * rows * (5 + key_frames) * tokens,
        ),
        name=f"attend{slot}",
    )(*scalars, table, *mine, *theirs)


def unpack_kernel(parts, per_part, *refs):
    count = parts * per_part
    pieces, out = refs[:count], refs[count]
    held, load_sem, store_sem = refs[count + 1 :]
    me = lax.axis_index("frm")
    loads, stores = [], []
    for at in range(count):
        loads.append(pltpu.make_async_copy(pieces[at], held.at[at], load_sem.at[at]))
        loads[-1].start()
    for at in range(count):
        slot, hop = at // parts, at % parts
        owner = lax.rem(me + parts - hop, parts)
        columns = pl.ds(pl.multiple_of((owner * per_part + slot) * DH, DH), DH)
        loads[at].wait()
        stores.append(pltpu.make_async_copy(held.at[at], out.at[:, :, columns], store_sem.at[at]))
        stores[-1].start()
    for copy in stores:
        copy.wait()


def unpack(parts, pieces):
    frames_dev, rows, _ = pieces[0].shape
    count = len(pieces)
    return pl.pallas_call(
        functools.partial(unpack_kernel, parts, count // parts),
        out_shape=jax.ShapeDtypeStruct((frames_dev, rows, count * DH), jnp.float32),
        in_specs=[pl.BlockSpec(memory_space=pl.ANY)] * count,
        out_specs=pl.BlockSpec(memory_space=pl.ANY),
        scratch_shapes=[
            pltpu.VMEM((count, frames_dev, rows, DH), jnp.float32),
            pltpu.SemaphoreType.DMA((count,)),
            pltpu.SemaphoreType.DMA((count,)),
        ],
        name="unpack",
    )(*pieces)


def around(value, hop):
    size = lax.axis_size("frm")
    return lax.ppermute(value, "frm", [(i, (i + hop) % size) for i in range(size)])


def swap(value):
    size = lax.axis_size("pos")
    return lax.ppermute(value, "pos", [(i, size - 1 - i) for i in range(size)])


def by_heads(queries, key_states, value_states, windows, strides, cutoffs):
    parts = lax.axis_size("frm")
    per_part = queries.shape[2] // DH // parts
    frames = queries.shape[0] * parts
    table = jnp.asarray(lowpass_table(frames))
    packed = [pack(slot, parts, queries, key_states, value_states) for slot in range(per_part)]
    moved = [[p[0]] + [around(p[hop], hop) for hop in range(1, parts)] for p in packed]
    pieces = []
    for slot, mine in enumerate(moved):
        theirs = [swap(piece) for piece in mine]
        done = attend_head(slot, parts, (windows, strides, cutoffs), table, mine, theirs)
        pieces += [done[0]] + [around(done[hop], hop) for hop in range(1, parts)]
    return unpack(parts, pieces)


def with_halo(value, sides, width):
    for axis, dim in sides:
        size, length = (lax.axis_size(axis), value.shape[dim])
        up = [(i, (i + 1) % size) for i in range(size - 1)]
        down = [(j, i) for i, j in up]
        last = lax.slice_in_dim(value, length - width, length, axis=dim)
        first = lax.slice_in_dim(value, 0, width, axis=dim)
        before = lax.ppermute(last, axis, up)
        after = lax.ppermute(first, axis, down)
        value = jnp.concatenate([before, value, after], axis=dim)
    return value


def attend(query_rows, key_rows, value_rows, allowed, score_scale):
    scores = (
        jnp.einsum("qhd,khd->hqk", query_rows, key_rows, precision=lax.Precision.HIGHEST)
        * score_scale
    )
    highest = jnp.max(jnp.where(allowed, scores, -1e30), axis=2, keepdims=True)
    weights = jnp.where(allowed, jnp.exp(scores - highest), 0.0)
    row_total = jnp.sum(weights, axis=2, keepdims=True)
    return jnp.einsum(
        "hqk,khd->qhd", weights / row_total, value_rows, precision=lax.Precision.HIGHEST
    )


def by_frames(queries, key_states, value_states, windows, strides, cutoffs):
    frames_dev, half_tokens, channels = queries.shape
    heads_local = channels // DH
    frame_groups = lax.axis_size("frm")
    pos_count = lax.axis_size("pos")
    total_frames = frames_dev * frame_groups
    halo_frames = frames_dev // 2
    score_scale = DH ** (-0.5)
    query_count = frames_dev * half_tokens
    query_rows = queries.reshape(query_count, heads_local, DH)
    query_blocks = queries.reshape(frames_dev, half_tokens, heads_local, DH)
    first_frame = lax.axis_index("frm") * frames_dev
    key_full, value_full = (
        lax.all_gather(key_states, "pos", axis=1, tiled=True),
        lax.all_gather(value_states, "pos", axis=1, tiled=True),
    )
    full_tokens = key_full.shape[1]
    stacked = jnp.stack([key_full, value_full])
    padded = with_halo(stacked, (("frm", 1),), halo_frames)
    window_span = 2 * halo_frames + 1
    span_rows = window_span * full_tokens
    span_offsets = jnp.arange(span_rows, dtype=jnp.int32) // full_tokens - halo_frames

    def local_frame(frame_local):
        query_part = lax.dynamic_index_in_dim(query_blocks, frame_local, 0, keepdims=False)
        block = lax.dynamic_slice_in_dim(padded, frame_local, window_span, 1)
        near_keys = block[0].reshape(span_rows, heads_local, DH)
        near_values = block[1].reshape(span_rows, heads_local, DH)
        near_frames = first_frame + frame_local + span_offsets
        inside = (near_frames >= 0) & (near_frames < total_frames)
        allowed = inside[None, None, :] & (
            jnp.abs(span_offsets)[None, None, :] <= windows[:, None, None]
        )
        return attend(query_part, near_keys, near_values, allowed, score_scale)

    local_out = lax.map(local_frame, jnp.arange(frames_dev, dtype=jnp.int32)).reshape(
        query_count, heads_local, DH
    )
    frame_keys = key_states[::KSTRIDE].reshape(-1, heads_local, DH)
    frame_values = value_states[::KSTRIDE].reshape(-1, heads_local, DH)
    rows_dev = frame_keys.shape[0]
    key_part = lax.all_gather(frame_keys, ("frm", "pos"), axis=0, tiled=True)
    value_part = lax.all_gather(frame_values, ("frm", "pos"), axis=0, tiled=True)
    row_count = key_part.shape[0]
    row_ids = jnp.arange(row_count, dtype=jnp.int32)
    frame_ids = (
        row_ids // rows_dev // pos_count * frames_dev + row_ids % rows_dev // half_tokens * KSTRIDE
    )
    allowed = (frame_ids[None, :] % strides[:, None] == 0)[:, None, :]
    scores = (
        jnp.einsum("qhd,khd->hqk", query_rows, key_part, precision=lax.Precision.HIGHEST)
        * score_scale
    )
    top_old = jnp.full((heads_local, query_count), -1e30, jnp.float32)
    top_new = jnp.maximum(top_old, jnp.max(jnp.where(allowed, scores, -1e30), axis=2))
    weights = jnp.where(allowed, jnp.exp(scores - top_new[:, :, None]), 0.0)
    total_new = jnp.sum(weights, axis=2)
    accum_new = jnp.einsum("hqk,khd->hqd", weights, value_part, precision=lax.Precision.HIGHEST)
    final_state = (top_new, total_new, accum_new)
    top_final, total_final, accum_final = final_state
    global_out = jnp.transpose(accum_final / total_final[:, :, None], (1, 0, 2))
    frequency = jnp.arange(total_frames, dtype=jnp.int32)
    phase_index = frequency[:, None] * frequency[None, :] % total_frames
    phases = 2.0 * math.pi / total_frames * phase_index.astype(jnp.float32)
    cos_table = jnp.cos(phases)
    sin_table = jnp.sin(phases)
    distance_freq = jnp.minimum(frequency, total_frames - frequency)
    low_keep = (distance_freq[None, :] <= cutoffs[:, None]).astype(jnp.float32)
    lowpass = (
        jnp.einsum("kf,hk,kg->hfg", cos_table, low_keep, cos_table, precision=lax.Precision.HIGHEST)
        + jnp.einsum(
            "kf,hk,kg->hfg", sin_table, low_keep, sin_table, precision=lax.Precision.HIGHEST
        )
    ) / total_frames
    group_items = half_tokens // frame_groups
    local_grid = local_out.reshape(frames_dev, frame_groups, group_items, channels)
    global_grid = global_out.reshape(frames_dev, frame_groups, group_items, channels)
    frame_block = lax.all_to_all(
        global_grid - local_grid, "frm", split_axis=1, concat_axis=0, tiled=True
    )
    frames_all = frame_block.shape[0]
    item_count = frame_block.shape[2]
    shaped = frame_block.reshape(frames_all, item_count, heads_local, DH)
    filtered_block = jnp.einsum(
        "hfg,gihd->fihd", lowpass, shaped, precision=lax.Precision.HIGHEST
    ).reshape(frame_block.shape)
    filtered = lax.all_to_all(filtered_block, "frm", split_axis=0, concat_axis=1, tiled=True)
    blended = local_grid + filtered
    return blended.reshape(frames_dev, half_tokens, channels)


def shards(queries, key_states, value_states, windows, strides, cutoffs):
    heads_local = queries.shape[2] // DH
    if heads_local % lax.axis_size("frm") == 0 and lax.axis_size("pos") == 2:
        return by_heads(queries, key_states, value_states, windows, strides, cutoffs)
    return by_frames(queries, key_states, value_states, windows, strides, cutoffs)


def solution(mesh):
    in_specs = (
        P(("grp", "frm"), "pos", "head"),
        P(("grp", "frm"), "pos", "head"),
        P(("grp", "frm"), "pos", "head"),
        P("head"),
        P("head"),
        P("head"),
    )
    out_specs = P(("grp", "frm"), "pos", "head")
    return jax.shard_map(shards, mesh=mesh, in_specs=in_specs, out_specs=out_specs, check_vma=False)
```

```python
import functools
import math

import jax
import jax.numpy as jnp
import numpy as np
from jax import lax
from jax.experimental import pallas as pl
from jax.experimental.pallas import tpu as pltpu
from jax.sharding import PartitionSpec as P


DH = 128
KSTRIDE = 4
WMAX = 2
MASKED = -1e30


def lowpass_table(frames):
    cutoff = np.arange(frames // 2 + 1)
    freq = np.arange(frames)
    keep = (np.minimum(freq, frames - freq)[None, :] <= cutoff[:, None]).astype(np.float64)
    waves = np.cos(2.0 * np.pi / frames * (np.outer(freq, freq) % frames))
    return (keep @ waves / frames).astype(np.float32)


def pack_kernel(slot, parts, per_part, *refs):
    sources, outs = refs[:3], refs[3 : 3 + parts]
    held, load_sem, store_sem = refs[3 + parts :]
    me = lax.axis_index("frm")
    order = [*range(1, parts), 0]
    loads, stores = {}, {}
    for hop in order:
        owner = lax.rem(me + hop, parts)
        columns = pl.ds(pl.multiple_of((owner * per_part + slot) * DH, DH), DH)
        for at in range(3):
            loads[hop, at] = pltpu.make_async_copy(
                sources[at].at[:, :, columns], held.at[hop, at], load_sem.at[hop, at]
            )
            loads[hop, at].start()
    for hop in order:
        for at in range(3):
            loads[hop, at].wait()
        stores[hop] = pltpu.make_async_copy(held.at[hop], outs[hop], store_sem.at[hop])
        stores[hop].start()
    for hop in order:
        stores[hop].wait()


def pack(slot, parts, queries, key_states, value_states):
    frames_dev, rows, channels = queries.shape
    piece = (3, frames_dev, rows, DH)
    moved = parts * math.prod(piece) * 4
    return pl.pallas_call(
        functools.partial(pack_kernel, slot, parts, channels // DH // parts),
        out_shape=[jax.ShapeDtypeStruct(piece, jnp.float32)] * parts,
        in_specs=[pl.BlockSpec(memory_space=pl.ANY)] * 3,
        out_specs=[pl.BlockSpec(memory_space=pl.ANY)] * parts,
        scratch_shapes=[
            pltpu.VMEM((parts, *piece), jnp.float32),
            pltpu.SemaphoreType.DMA((parts, 3)),
            pltpu.SemaphoreType.DMA((parts,)),
        ],
        cost_estimate=pl.CostEstimate(flops=0, bytes_accessed=2 * moved, transcendentals=0),
    )(queries, key_states, value_states)


def split(value):
    high = value.astype(jnp.bfloat16)
    return high, (value - high.astype(jnp.float32)).astype(jnp.bfloat16)


def weighted(scores, values):
    highest = jnp.max(scores, axis=1, keepdims=True)
    weights = jnp.exp(scores - highest)
    total = jnp.sum(weights, axis=1, keepdims=True)
    high, low = split(weights)
    wide = jnp.dot(high, values, preferred_element_type=jnp.float32)
    rest = jnp.dot(low, values[:, :DH], preferred_element_type=jnp.float32)
    return (wide[:, :DH] + wide[:, DH:] + rest) / total


def attend_kernel(slot, parts, per_part, *refs):
    windows, strides, cutoffs, table = refs[:4]
    mine, theirs = refs[4 : 4 + parts], refs[4 + parts : 4 + 2 * parts]
    outs = refs[4 + 2 * parts : 4 + 3 * parts]
    (q_in, k_in, v_in, q_cat, k_cat, v_cat, kg_cat, vg_cat, local, diff, load_sem, store_sem) = refs[
        4 + 3 * parts :
    ]
    frames, rows, _ = q_in.shape
    tokens = k_in.shape[1]
    frames_dev = frames // parts
    me = lax.axis_index("frm")
    head = me * per_part + slot
    window, stride, cutoff = windows[head], strides[head], cutoffs[head]

    loads = []
    for hop in range(parts):
        owner = lax.rem(me + parts - hop, parts)
        span = pl.ds(owner * frames_dev, frames_dev)
        near, far = pl.ds(0, rows), pl.ds(rows, rows)
        for at, (source, target) in enumerate(
            (
                (mine[hop].at[0], q_in.at[span]),
                (mine[hop].at[1], k_in.at[span, near]),
                (mine[hop].at[2], v_in.at[span, near]),
                (theirs[hop].at[1], k_in.at[span, far]),
                (theirs[hop].at[2], v_in.at[span, far]),
            )
        ):
            copy = pltpu.make_async_copy(source, target, load_sem.at[hop, at])
            copy.start()
            loads.append(copy)
    for copy in loads:
        copy.wait()

    score_scale = DH ** (-0.5)

    def prepare(frame, carry):
        q_at = pl.ds(pl.multiple_of(frame * rows, rows), rows)
        k_at = pl.ds(pl.multiple_of(frame * tokens, tokens), tokens)
        high, low = split(q_in[frame] * score_scale)
        q_cat[q_at, 0:DH] = high
        q_cat[q_at, DH : 2 * DH] = low
        q_cat[q_at, 2 * DH : 3 * DH] = high
        k_high, k_low = split(k_in[frame])
        k_cat[k_at, 0:DH] = k_high
        k_cat[k_at, DH : 2 * DH] = k_high
        k_cat[k_at, 2 * DH : 3 * DH] = k_low
        v_high, v_low = split(v_in[frame])
        v_cat[k_at, 0:DH] = v_high
        v_cat[k_at, DH : 2 * DH] = v_low
        return carry

    lax.fori_loop(0, frames, prepare, 0)
    key_frames = frames // KSTRIDE
    for at in range(key_frames):
        source = pl.ds(at * KSTRIDE * tokens, tokens)
        target = pl.ds(at * tokens, tokens)
        kg_cat[target, :] = k_cat[source, :]
        vg_cat[target, :] = v_cat[source, :]

    def scores_of(query_rows, key_rows):
        return lax.dot_general(
            query_rows, key_rows, (((1,), (1,)), ((), ())), preferred_element_type=jnp.float32
        )

    pair = 2
    reach = min(2 * WMAX + pair, frames)
    pair_rows = pair * rows
    key_frame = lax.broadcasted_iota(jnp.int32, (1, key_frames * tokens), 1) // tokens * KSTRIDE
    global_bias = jnp.where(lax.rem(key_frame, stride) == 0, 0.0, MASKED)

    def per_pair(step, carry):
        first = step * pair
        start = jnp.clip(first - WMAX, 0, frames - reach)
        q_part = q_cat[pl.ds(pl.multiple_of(first * rows, pair_rows), pair_rows), :]
        k_at = pl.ds(pl.multiple_of(start * tokens, tokens), reach * tokens)
        near_frame = start + lax.broadcasted_iota(jnp.int32, (pair_rows, reach * tokens), 1) // tokens
        query_frame = first + lax.broadcasted_iota(jnp.int32, (pair_rows, reach * tokens), 0) // rows
        scores = scores_of(q_part, k_cat[k_at, :])
        scores = jnp.where(jnp.abs(near_frame - query_frame) <= window, scores, MASKED)
        local_part = weighted(scores, v_cat[k_at, :])
        global_part = weighted(scores_of(q_part, kg_cat[...]) + global_bias, vg_cat[...])
        difference = global_part - local_part
        for at in range(pair):
            local[first + at] = local_part[at * rows : (at + 1) * rows]
            diff[first + at] = difference[at * rows : (at + 1) * rows]
        return carry

    lax.fori_loop(0, frames // pair, per_pair, 0)

    kept = jnp.clip(cutoff, 0, frames // 2)

    def blend(frame, carry):
        total = local[frame]
        for other in range(frames):
            total += table[kept, lax.rem(frame + frames - other, frames)] * diff[other]
        q_in[frame] = total
        return carry

    lax.fori_loop(0, frames, blend, 0)
    stores = []
    for hop in range(parts):
        owner = lax.rem(me + hop, parts)
        stores.append(
            pltpu.make_async_copy(
                q_in.at[pl.ds(owner * frames_dev, frames_dev)], outs[hop], store_sem.at[hop]
            )
        )
        stores[-1].start()
    for copy in stores:
        copy.wait()


def attend_head(slot, parts, scalars, table, mine, theirs):
    _, frames_dev, rows, _ = mine[0].shape
    frames, tokens = frames_dev * parts, 2 * rows
    per_part = scalars[0].shape[0] // parts
    key_frames = frames // KSTRIDE
    flops = 12 * frames * rows * (5 + key_frames) * tokens * DH
    return pl.pallas_call(
        functools.partial(attend_kernel, slot, parts, per_part),
        out_shape=[jax.ShapeDtypeStruct((frames_dev, rows, DH), jnp.float32)] * parts,
        in_specs=[pl.BlockSpec(memory_space=pltpu.SMEM)] * 4
        + [pl.BlockSpec(memory_space=pl.ANY)] * (2 * parts),
        out_specs=[pl.BlockSpec(memory_space=pl.ANY)] * parts,
        scratch_shapes=[
            pltpu.VMEM((frames, rows, DH), jnp.float32),
            pltpu.VMEM((frames, tokens, DH), jnp.float32),
            pltpu.VMEM((frames, tokens, DH), jnp.float32),
            pltpu.VMEM((frames * rows, 3 * DH), jnp.bfloat16),
            pltpu.VMEM((frames * tokens, 3 * DH), jnp.bfloat16),
            pltpu.VMEM((frames * tokens, 2 * DH), jnp.bfloat16),
            pltpu.VMEM((key_frames * tokens, 3 * DH), jnp.bfloat16),
            pltpu.VMEM((key_frames * tokens, 2 * DH), jnp.bfloat16),
            pltpu.VMEM((frames, rows, DH), jnp.float32),
            pltpu.VMEM((frames, rows, DH), jnp.float32),
            pltpu.SemaphoreType.DMA((parts, 5)),
            pltpu.SemaphoreType.DMA((parts,)),
        ],
        cost_estimate=pl.CostEstimate(
            flops=flops,
            bytes_accessed=6 * frames * rows * DH * 4,
            transcendentals=frames * rows * (5 + key_frames) * tokens,
        ),
    )(*scalars, table, *mine, *theirs)


def unpack_kernel(parts, per_part, *refs):
    count = parts * per_part
    pieces, out = refs[:count], refs[count]
    held, load_sem, store_sem = refs[count + 1 :]
    me = lax.axis_index("frm")
    loads, stores = [], []
    for at in range(count):
        loads.append(pltpu.make_async_copy(pieces[at], held.at[at], load_sem.at[at]))
        loads[-1].start()
    for at in range(count):
        slot, hop = at // parts, at % parts
        owner = lax.rem(me + parts - hop, parts)
        columns = pl.ds(pl.multiple_of((owner * per_part + slot) * DH, DH), DH)
        loads[at].wait()
        stores.append(pltpu.make_async_copy(held.at[at], out.at[:, :, columns], store_sem.at[at]))
        stores[-1].start()
    for copy in stores:
        copy.wait()


def unpack(parts, pieces):
    frames_dev, rows, _ = pieces[0].shape
    count = len(pieces)
    return pl.pallas_call(
        functools.partial(unpack_kernel, parts, count // parts),
        out_shape=jax.ShapeDtypeStruct((frames_dev, rows, count * DH), jnp.float32),
        in_specs=[pl.BlockSpec(memory_space=pl.ANY)] * count,
        out_specs=pl.BlockSpec(memory_space=pl.ANY),
        scratch_shapes=[
            pltpu.VMEM((count, frames_dev, rows, DH), jnp.float32),
            pltpu.SemaphoreType.DMA((count,)),
            pltpu.SemaphoreType.DMA((count,)),
        ],
        name="unpack",
    )(*pieces)


def around(value, hop):
    size = lax.axis_size("frm")
    return lax.ppermute(value, "frm", [(i, (i + hop) % size) for i in range(size)])


def swap(value):
    size = lax.axis_size("pos")
    return lax.ppermute(value, "pos", [(i, size - 1 - i) for i in range(size)])


def by_heads(queries, key_states, value_states, windows, strides, cutoffs):
    parts = lax.axis_size("frm")
    per_part = queries.shape[2] // DH // parts
    frames = queries.shape[0] * parts
    table = jnp.asarray(lowpass_table(frames))
    scalars = (windows, strides, cutoffs)
    packed, sources, moved, pieces = [], (queries, key_states, value_states), [], []
    for slot in range(per_part):
        packed.append(pack(slot, parts, *sources))
        packed[-1], sources = lax.optimization_barrier((packed[-1], sources))
        moved.append([packed[-1][0]])
        for hop in range(1, parts):
            moved[-1].append(around(packed[-1][hop], hop))
    for slot, mine in enumerate(moved):
        theirs = []
        for hop in range(parts):
            theirs.append(swap(mine[hop]))
        done = attend_head(slot, parts, scalars, table, mine, theirs)
        pieces.append(done[0])
        for hop in range(1, parts):
            pieces.append(around(done[hop], hop))
    return unpack(parts, pieces)


def with_halo(value, sides, width):
    for axis, dim in sides:
        size, length = (lax.axis_size(axis), value.shape[dim])
        up = [(i, (i + 1) % size) for i in range(size - 1)]
        down = [(j, i) for i, j in up]
        last = lax.slice_in_dim(value, length - width, length, axis=dim)
        first = lax.slice_in_dim(value, 0, width, axis=dim)
        before = lax.ppermute(last, axis, up)
        after = lax.ppermute(first, axis, down)
        value = jnp.concatenate([before, value, after], axis=dim)
    return value


def attend(query_rows, key_rows, value_rows, allowed, score_scale):
    scores = (
        jnp.einsum("qhd,khd->hqk", query_rows, key_rows, precision=lax.Precision.HIGHEST)
        * score_scale
    )
    highest = jnp.max(jnp.where(allowed, scores, -1e30), axis=2, keepdims=True)
    weights = jnp.where(allowed, jnp.exp(scores - highest), 0.0)
    row_total = jnp.sum(weights, axis=2, keepdims=True)
    return jnp.einsum(
        "hqk,khd->qhd", weights / row_total, value_rows, precision=lax.Precision.HIGHEST
    )


def by_frames(queries, key_states, value_states, windows, strides, cutoffs):
    frames_dev, half_tokens, channels = queries.shape
    heads_local = channels // DH
    frame_groups = lax.axis_size("frm")
    pos_count = lax.axis_size("pos")
    total_frames = frames_dev * frame_groups
    halo_frames = frames_dev // 2
    score_scale = DH ** (-0.5)
    query_count = frames_dev * half_tokens
    query_rows = queries.reshape(query_count, heads_local, DH)
    query_blocks = queries.reshape(frames_dev, half_tokens, heads_local, DH)
    first_frame = lax.axis_index("frm") * frames_dev
    key_full, value_full = (
        lax.all_gather(key_states, "pos", axis=1, tiled=True),
        lax.all_gather(value_states, "pos", axis=1, tiled=True),
    )
    full_tokens = key_full.shape[1]
    stacked = jnp.stack([key_full, value_full])
    padded = with_halo(stacked, (("frm", 1),), halo_frames)
    window_span = 2 * halo_frames + 1
    span_rows = window_span * full_tokens
    span_offsets = jnp.arange(span_rows, dtype=jnp.int32) // full_tokens - halo_frames

    def local_frame(frame_local):
        query_part = lax.dynamic_index_in_dim(query_blocks, frame_local, 0, keepdims=False)
        block = lax.dynamic_slice_in_dim(padded, frame_local, window_span, 1)
        near_keys = block[0].reshape(span_rows, heads_local, DH)
        near_values = block[1].reshape(span_rows, heads_local, DH)
        near_frames = first_frame + frame_local + span_offsets
        inside = (near_frames >= 0) & (near_frames < total_frames)
        allowed = inside[None, None, :] & (
            jnp.abs(span_offsets)[None, None, :] <= windows[:, None, None]
        )
        return attend(query_part, near_keys, near_values, allowed, score_scale)

    local_out = lax.map(local_frame, jnp.arange(frames_dev, dtype=jnp.int32)).reshape(
        query_count, heads_local, DH
    )
    frame_keys = key_states[::KSTRIDE].reshape(-1, heads_local, DH)
    frame_values = value_states[::KSTRIDE].reshape(-1, heads_local, DH)
    rows_dev = frame_keys.shape[0]
    key_part = lax.all_gather(frame_keys, ("frm", "pos"), axis=0, tiled=True)
    value_part = lax.all_gather(frame_values, ("frm", "pos"), axis=0, tiled=True)
    row_count = key_part.shape[0]
    row_ids = jnp.arange(row_count, dtype=jnp.int32)
    frame_ids = (
        row_ids // rows_dev // pos_count * frames_dev + row_ids % rows_dev // half_tokens * KSTRIDE
    )
    allowed = (frame_ids[None, :] % strides[:, None] == 0)[:, None, :]
    scores = (
        jnp.einsum("qhd,khd->hqk", query_rows, key_part, precision=lax.Precision.HIGHEST)
        * score_scale
    )
    top_old = jnp.full((heads_local, query_count), -1e30, jnp.float32)
    top_new = jnp.maximum(top_old, jnp.max(jnp.where(allowed, scores, -1e30), axis=2))
    weights = jnp.where(allowed, jnp.exp(scores - top_new[:, :, None]), 0.0)
    total_new = jnp.sum(weights, axis=2)
    accum_new = jnp.einsum("hqk,khd->hqd", weights, value_part, precision=lax.Precision.HIGHEST)
    final_state = (top_new, total_new, accum_new)
    _, total_final, accum_final = final_state
    global_out = jnp.transpose(accum_final / total_final[:, :, None], (1, 0, 2))
    frequency = jnp.arange(total_frames, dtype=jnp.int32)
    phase_index = frequency[:, None] * frequency[None, :] % total_frames
    phases = 2.0 * math.pi / total_frames * phase_index.astype(jnp.float32)
    cos_table = jnp.cos(phases)
    sin_table = jnp.sin(phases)
    distance_freq = jnp.minimum(frequency, total_frames - frequency)
    low_keep = (distance_freq[None, :] <= cutoffs[:, None]).astype(jnp.float32)
    lowpass = (
        jnp.einsum("kf,hk,kg->hfg", cos_table, low_keep, cos_table, precision=lax.Precision.HIGHEST)
        + jnp.einsum(
            "kf,hk,kg->hfg", sin_table, low_keep, sin_table, precision=lax.Precision.HIGHEST
        )
    ) / total_frames
    group_items = half_tokens // frame_groups
    local_grid = local_out.reshape(frames_dev, frame_groups, group_items, channels)
    global_grid = global_out.reshape(frames_dev, frame_groups, group_items, channels)
    frame_block = lax.all_to_all(
        global_grid - local_grid, "frm", split_axis=1, concat_axis=0, tiled=True
    )
    frames_all = frame_block.shape[0]
    item_count = frame_block.shape[2]
    shaped = frame_block.reshape(frames_all, item_count, heads_local, DH)
    filtered_block = jnp.einsum(
        "hfg,gihd->fihd", lowpass, shaped, precision=lax.Precision.HIGHEST
    ).reshape(frame_block.shape)
    filtered = lax.all_to_all(filtered_block, "frm", split_axis=0, concat_axis=1, tiled=True)
    blended = local_grid + filtered
    return blended.reshape(frames_dev, half_tokens, channels)


def splits_by_heads(heads_local, parts, pos_count):
    return heads_local % parts == 0 and pos_count == 2


def shards(queries, key_states, value_states, windows, strides, cutoffs):
    heads_local = queries.shape[2] // DH
    if splits_by_heads(heads_local, lax.axis_size("frm"), lax.axis_size("pos")):
        return by_heads(queries, key_states, value_states, windows, strides, cutoffs)
    return by_frames(queries, key_states, value_states, windows, strides, cutoffs)


def solution(mesh):
    in_specs = (
        P(("grp", "frm"), "pos", "head"),
        P(("grp", "frm"), "pos", "head"),
        P(("grp", "frm"), "pos", "head"),
        P("head"),
        P("head"),
        P("head"),
    )
    out_specs = P(("grp", "frm"), "pos", "head")
    return jax.shard_map(
        shards, mesh=mesh, in_specs=in_specs, out_specs=out_specs, check_vma=False
    )
```

```python
import functools
import math

import jax
import jax.numpy as jnp
import numpy as np
from jax import lax
from jax.experimental import pallas as pl
from jax.experimental.pallas import tpu as pltpu
from jax.sharding import PartitionSpec as P


DH = 128
KSTRIDE = 4
WMAX = 2
MASKED = -1e30
GROUP = 4
ATTEND_VMEM = 24 * 2**20
BLEND = 8


def lowpass_table(frames):
    cutoff = np.arange(frames // 2 + 1)
    freq = np.arange(frames)
    keep = (np.minimum(freq, frames - freq)[None, :] <= cutoff[:, None]).astype(np.float64)
    waves = np.cos(2.0 * np.pi / frames * (np.outer(freq, freq) % frames))
    return (keep @ waves / frames).astype(np.float32)


def wires(parts):
    return sorted(range(1, parts), key=lambda hop: (hop.bit_count() % 2 == 0, -hop))


def pack_kernel(slot, parts, per_part, *refs):
    sources, outs = refs[:3], refs[3 : 3 + parts]
    held, load_sem, store_sem = refs[3 + parts :]
    me = lax.axis_index("frm")
    order = [*wires(parts), 0]
    loads, stores = {}, {}
    for hop in order:
        owner = lax.bitwise_xor(me, hop)
        columns = pl.ds(pl.multiple_of((owner * per_part + slot) * DH, DH), DH)
        for at in range(3):
            loads[hop, at] = pltpu.make_async_copy(
                sources[at].at[:, :, columns], held.at[hop, at], load_sem.at[hop, at]
            )
            loads[hop, at].start()
    for hop in order:
        for at in range(3):
            loads[hop, at].wait()
        stores[hop] = pltpu.make_async_copy(held.at[hop], outs[hop], store_sem.at[hop])
        stores[hop].start()
    for hop in order:
        stores[hop].wait()


def pack(slot, parts, queries, key_states, value_states):
    frames_dev, rows, channels = queries.shape
    piece = (3, frames_dev, rows, DH)
    moved = parts * math.prod(piece) * 4
    return pl.pallas_call(
        functools.partial(pack_kernel, slot, parts, channels // DH // parts),
        out_shape=[jax.ShapeDtypeStruct(piece, jnp.float32)] * parts,
        in_specs=[pl.BlockSpec(memory_space=pl.ANY)] * 3,
        out_specs=[pl.BlockSpec(memory_space=pl.ANY)] * parts,
        scratch_shapes=[
            pltpu.VMEM((parts, *piece), jnp.float32),
            pltpu.SemaphoreType.DMA((parts, 3)),
            pltpu.SemaphoreType.DMA((parts,)),
        ],
        cost_estimate=pl.CostEstimate(flops=0, bytes_accessed=2 * moved, transcendentals=0),
    )(queries, key_states, value_states)


def split(value):
    high = value.astype(jnp.bfloat16)
    return high, (value - high.astype(jnp.float32)).astype(jnp.bfloat16)


def attend_kernel(slot, parts, per_part, riders, *refs):
    windows, strides, cutoffs, table = refs[:4]
    refs = refs[4:]
    mine, theirs, refs = refs[:parts], refs[parts : 2 * parts], refs[2 * parts :]
    earlier, refs = (refs[:parts], refs[parts:]) if riders else ((), refs)
    outs, refs = refs[:parts], refs[parts:]
    (q_in, k_in, v_in, q_cat, k_cat, v_cat, kg_cat, vg_cat, local, diff, load_sem, store_sem) = refs[
        :12
    ]
    frames, rows, _ = q_in.shape
    tokens = k_in.shape[1]
    frames_dev = frames // parts
    me = lax.axis_index("frm")
    head = me * per_part + slot
    window, stride, cutoff = windows[head], strides[head], cutoffs[head]

    loads = []
    for hop in range(parts):
        owner = lax.bitwise_xor(me, hop)
        span = pl.ds(owner * frames_dev, frames_dev)
        near, far = pl.ds(0, rows), pl.ds(rows, rows)
        loads.append([])
        for at, (source, target) in enumerate(
            (
                (mine[hop].at[0], q_in.at[span]),
                (mine[hop].at[1], k_in.at[span, near]),
                (theirs[hop].at[1], k_in.at[span, far]),
                (mine[hop].at[2], v_in.at[span, near]),
                (theirs[hop].at[2], v_in.at[span, far]),
            )
        ):
            copy = pltpu.make_async_copy(source, target, load_sem.at[hop, at])
            copy.start()
            loads[-1].append(copy)

    if riders:
        held, ride_sem = refs[12:]
        rides = [
            pltpu.make_async_copy(earlier[hop], held.at[hop], ride_sem.at[0, hop])
            for hop in range(parts)
        ]
        for copy in rides:
            copy.start()

    score_scale = DH ** (-0.5) * math.log2(math.e)

    def prepare(frame, carry):
        q_at = pl.ds(pl.multiple_of(frame * rows, rows), rows)
        k_at = pl.ds(pl.multiple_of(frame * tokens, tokens), tokens)
        high, low = split(q_in[frame] * score_scale)
        q_cat[q_at, 0:DH] = high
        q_cat[q_at, DH : 2 * DH] = low
        q_cat[q_at, 2 * DH : 3 * DH] = high
        k_high, k_low = split(k_in[frame])
        k_cat[k_at, 0:DH] = k_high
        k_cat[k_at, DH : 2 * DH] = k_high
        k_cat[k_at, 2 * DH : 3 * DH] = k_low
        v_high, v_low = split(v_in[frame].T)
        v_cat[0:DH, k_at] = v_high
        v_cat[DH : 2 * DH, k_at] = v_low
        return carry

    for hop in range(parts):
        owner = lax.bitwise_xor(me, hop)
        for copy in loads[hop]:
            copy.wait()
        lax.fori_loop(owner * frames_dev, (owner + 1) * frames_dev, prepare, 0)
    key_frames = frames // KSTRIDE
    for at in range(key_frames):
        source = pl.ds(at * KSTRIDE * tokens, tokens)
        target = pl.ds(at * tokens, tokens)
        kg_cat[target, :] = k_cat[source, :]
        vg_cat[:, target] = v_cat[:, source]

    group = GROUP
    reach = min(2 * WMAX + group, frames)
    group_rows = group * rows
    lane_frame = lax.broadcasted_iota(jnp.int32, (1, group_rows), 1) // rows

    def weighted(key_rows, bias, value_columns, query_rows):
        scores = lax.dot_general(
            key_rows, query_rows, (((1,), (1,)), ((), ())), preferred_element_type=jnp.float32
        )
        parts_of = [scores[at * tokens : (at + 1) * tokens] for at in range(len(bias))]
        peaks = [
            jnp.max(part, axis=0, keepdims=True) + shift for part, shift in zip(parts_of, bias)
        ]
        highest = functools.reduce(jnp.maximum, peaks)
        weights = jnp.concatenate(
            [jnp.exp2(part - (highest - shift)) for part, shift in zip(parts_of, bias)], axis=0
        )
        total = jnp.sum(weights, axis=0, keepdims=True)
        high, low = split(weights)
        wide = jnp.dot(value_columns, high, preferred_element_type=jnp.float32)
        rest = jnp.dot(value_columns[:DH], low, preferred_element_type=jnp.float32)
        return (wide[:DH] + wide[DH:] + rest) / total

    global_bias = [
        jnp.where(lax.rem(at * KSTRIDE, stride) == 0, 0.0, MASKED) for at in range(key_frames)
    ]

    def per_group(step, carry):
        first = step * group
        start = jnp.clip(first - WMAX, 0, frames - reach)
        q_part = q_cat[pl.ds(pl.multiple_of(first * rows, group_rows), group_rows), :]
        k_at = pl.ds(pl.multiple_of(start * tokens, tokens), reach * tokens)
        local_bias = [
            jnp.where(jnp.abs(start + at - first - lane_frame) <= window, 0.0, MASKED)
            for at in range(reach)
        ]
        local_part = weighted(k_cat[k_at, :], local_bias, v_cat[:, k_at], q_part)
        global_part = weighted(kg_cat[...], global_bias, vg_cat[...], q_part)
        difference = (global_part - local_part).T
        local_part = local_part.T
        for at in range(group):
            local[first + at] = local_part[at * rows : (at + 1) * rows]
            diff[first + at] = difference[at * rows : (at + 1) * rows]
        return carry

    lax.fori_loop(0, frames // group, per_group, 0)

    stores = []
    for hop in range(parts if riders else 0):
        rides[hop].wait()
        stores.append(
            pltpu.make_async_copy(held.at[hop], outs[hop].at[0:riders], ride_sem.at[1, hop])
        )
        stores[-1].start()

    half = frames // 2
    kept = jnp.clip(cutoff, 0, half)
    even = [0.5 * (table[kept, at] + table[kept, at + half]) for at in range(half)]
    odd = [0.5 * (table[kept, at] - table[kept, at + half]) for at in range(half)]

    def blend(row, carry):
        at = pl.ds(pl.multiple_of(row * BLEND, BLEND), BLEND)
        first = [diff[frame, at] for frame in range(half)]
        second = [diff[frame + half, at] for frame in range(half)]
        sums = [x + y for x, y in zip(first, second)]
        gaps = [x - y for x, y in zip(first, second)]
        for frame in range(half):
            periodic = sum(even[(frame - other) % half] * sums[other] for other in range(half))
            turning = sum(
                (odd[frame - other] if other <= frame else -odd[frame - other + half]) * gaps[other]
                for other in range(half)
            )
            q_in[frame, at] = local[frame, at] + (periodic + turning)
            q_in[frame + half, at] = local[frame + half, at] + (periodic - turning)
        return carry

    lax.fori_loop(0, rows // BLEND, blend, 0)
    for hop in range(parts):
        owner = lax.bitwise_xor(me, hop)
        stores.append(
            pltpu.make_async_copy(
                q_in.at[pl.ds(owner * frames_dev, frames_dev)], outs[hop].at[riders], store_sem.at[hop]
            )
        )
        stores[-1].start()
    for copy in stores:
        copy.wait()


def attend_head(slot, parts, scalars, table, mine, theirs, earlier):
    _, frames_dev, rows, _ = mine[0].shape
    frames, tokens = frames_dev * parts, 2 * rows
    per_part = scalars[0].shape[0] // parts
    key_frames = frames // KSTRIDE
    riders = earlier[0].shape[0] if earlier else 0
    result = (riders + 1, frames_dev, rows, DH)
    scratch = []
    if riders:
        scratch = [
            pltpu.VMEM((parts, riders, frames_dev, rows, DH), jnp.float32),
            pltpu.SemaphoreType.DMA((2, parts)),
        ]
    flops = 12 * frames * rows * (5 + key_frames) * tokens * DH
    return pl.pallas_call(
        functools.partial(attend_kernel, slot, parts, per_part, riders),
        out_shape=[jax.ShapeDtypeStruct(result, jnp.float32)] * parts,
        in_specs=[pl.BlockSpec(memory_space=pltpu.SMEM)] * 4
        + [pl.BlockSpec(memory_space=pl.ANY)] * (2 * parts + len(earlier)),
        out_specs=[pl.BlockSpec(memory_space=pl.ANY)] * parts,
        scratch_shapes=[
            pltpu.VMEM((frames, rows, DH), jnp.float32),
            pltpu.VMEM((frames, tokens, DH), jnp.float32),
            pltpu.VMEM((frames, tokens, DH), jnp.float32),
            pltpu.VMEM((frames * rows, 3 * DH), jnp.bfloat16),
            pltpu.VMEM((frames * tokens, 3 * DH), jnp.bfloat16),
            pltpu.VMEM((2 * DH, frames * tokens), jnp.bfloat16),
            pltpu.VMEM((key_frames * tokens, 3 * DH), jnp.bfloat16),
            pltpu.VMEM((2 * DH, key_frames * tokens), jnp.bfloat16),
            pltpu.VMEM((frames, rows, DH), jnp.float32),
            pltpu.VMEM((frames, rows, DH), jnp.float32),
            pltpu.SemaphoreType.DMA((parts, 5)),
            pltpu.SemaphoreType.DMA((parts,)),
        ]
        + scratch,
        cost_estimate=pl.CostEstimate(
            flops=flops,
            bytes_accessed=6 * frames * rows * DH * 4,
            transcendentals=frames * rows * (5 + key_frames) * tokens,
        ),
        compiler_params=pltpu.CompilerParams(vmem_limit_bytes=ATTEND_VMEM),
    )(*scalars, table, *mine, *theirs, *earlier)


def unpack_kernel(parts, per_part, first, *refs):
    pieces, refs = refs[:parts], refs[parts:]
    out, held, load_sem, store_sem = refs[-4:]
    slots = held.shape[1]
    me = lax.axis_index("frm")
    loads, stores = [], []
    for hop in range(parts):
        loads.append(pltpu.make_async_copy(pieces[hop], held.at[hop], load_sem.at[hop]))
        loads[-1].start()
    for hop in range(parts):
        owner = lax.bitwise_xor(me, hop)
        loads[hop].wait()
        for at in range(slots):
            columns = pl.ds(pl.multiple_of((owner * per_part + first + at) * DH, DH), DH)
            stores.append(
                pltpu.make_async_copy(held.at[hop, at], out.at[:, :, columns], store_sem.at[hop, at])
            )
            stores[-1].start()
    for copy in stores:
        copy.wait()


def unpack(parts, per_part, first, pieces, out=None):
    slots, frames_dev, rows, _ = pieces[0].shape
    operands = list(pieces) if out is None else [*pieces, out]
    return pl.pallas_call(
        functools.partial(unpack_kernel, parts, per_part, first),
        out_shape=jax.ShapeDtypeStruct((frames_dev, rows, parts * per_part * DH), jnp.float32),
        in_specs=[pl.BlockSpec(memory_space=pl.ANY)] * len(operands),
        out_specs=pl.BlockSpec(memory_space=pl.ANY),
        scratch_shapes=[
            pltpu.VMEM((parts, slots, frames_dev, rows, DH), jnp.float32),
            pltpu.SemaphoreType.DMA((parts,)),
            pltpu.SemaphoreType.DMA((parts, slots)),
        ],
        input_output_aliases={} if out is None else {parts: 0},
    )(*operands)


def around(value, hop):
    size = lax.axis_size("frm")
    return lax.ppermute(value, "frm", [(i, i ^ hop) for i in range(size)])


def swap(value):
    size = lax.axis_size("pos")
    return lax.ppermute(value, "pos", [(i, size - 1 - i) for i in range(size)])


def by_heads(queries, key_states, value_states, windows, strides, cutoffs):
    parts = lax.axis_size("frm")
    per_part = queries.shape[2] // DH // parts
    frames = queries.shape[0] * parts
    table = jnp.asarray(lowpass_table(frames))
    scalars = (windows, strides, cutoffs)
    packed, sources, moved = [], (queries, key_states, value_states), []
    for slot in range(per_part):
        packed.append(pack(slot, parts, *sources))
        packed[-1], sources = lax.optimization_barrier((packed[-1], sources))
        moved.append([packed[-1][0]] + [None] * (parts - 1))
        for hop in wires(parts):
            moved[-1][hop] = around(packed[-1][hop], hop)
    earlier, out, first = (), None, 0
    for slot, mine in enumerate(moved):
        theirs = []
        for hop in range(parts):
            theirs.append(swap(mine[hop]))
        done = attend_head(slot, parts, scalars, table, mine, theirs, earlier)
        if slot < per_part - 2:
            earlier = done
            continue
        earlier, landed = (), [done[0]] + [None] * (parts - 1)
        for hop in wires(parts):
            landed[hop] = around(done[hop], hop)
        out = unpack(parts, per_part, first, landed, out)
        first = slot + 1
    return out


def with_halo(value, sides, width):
    for axis, dim in sides:
        size, length = (lax.axis_size(axis), value.shape[dim])
        up = [(i, (i + 1) % size) for i in range(size - 1)]
        down = [(j, i) for i, j in up]
        last = lax.slice_in_dim(value, length - width, length, axis=dim)
        first = lax.slice_in_dim(value, 0, width, axis=dim)
        before = lax.ppermute(last, axis, up)
        after = lax.ppermute(first, axis, down)
        value = jnp.concatenate([before, value, after], axis=dim)
    return value


def attend(query_rows, key_rows, value_rows, allowed, score_scale):
    scores = (
        jnp.einsum("qhd,khd->hqk", query_rows, key_rows, precision=lax.Precision.HIGHEST)
        * score_scale
    )
    highest = jnp.max(jnp.where(allowed, scores, -1e30), axis=2, keepdims=True)
    weights = jnp.where(allowed, jnp.exp(scores - highest), 0.0)
    row_total = jnp.sum(weights, axis=2, keepdims=True)
    return jnp.einsum(
        "hqk,khd->qhd", weights / row_total, value_rows, precision=lax.Precision.HIGHEST
    )


def by_frames(queries, key_states, value_states, windows, strides, cutoffs):
    frames_dev, half_tokens, channels = queries.shape
    heads_local = channels // DH
    frame_groups = lax.axis_size("frm")
    pos_count = lax.axis_size("pos")
    total_frames = frames_dev * frame_groups
    halo_frames = frames_dev // 2
    score_scale = DH ** (-0.5)
    query_count = frames_dev * half_tokens
    query_rows = queries.reshape(query_count, heads_local, DH)
    query_blocks = queries.reshape(frames_dev, half_tokens, heads_local, DH)
    first_frame = lax.axis_index("frm") * frames_dev
    key_full, value_full = (
        lax.all_gather(key_states, "pos", axis=1, tiled=True),
        lax.all_gather(value_states, "pos", axis=1, tiled=True),
    )
    full_tokens = key_full.shape[1]
    stacked = jnp.stack([key_full, value_full])
    padded = with_halo(stacked, (("frm", 1),), halo_frames)
    window_span = 2 * halo_frames + 1
    span_rows = window_span * full_tokens
    span_offsets = jnp.arange(span_rows, dtype=jnp.int32) // full_tokens - halo_frames

    def local_frame(frame_local):
        query_part = lax.dynamic_index_in_dim(query_blocks, frame_local, 0, keepdims=False)
        block = lax.dynamic_slice_in_dim(padded, frame_local, window_span, 1)
        near_keys = block[0].reshape(span_rows, heads_local, DH)
        near_values = block[1].reshape(span_rows, heads_local, DH)
        near_frames = first_frame + frame_local + span_offsets
        inside = (near_frames >= 0) & (near_frames < total_frames)
        allowed = inside[None, None, :] & (
            jnp.abs(span_offsets)[None, None, :] <= windows[:, None, None]
        )
        return attend(query_part, near_keys, near_values, allowed, score_scale)

    local_out = lax.map(local_frame, jnp.arange(frames_dev, dtype=jnp.int32)).reshape(
        query_count, heads_local, DH
    )
    frame_keys = key_states[::KSTRIDE].reshape(-1, heads_local, DH)
    frame_values = value_states[::KSTRIDE].reshape(-1, heads_local, DH)
    rows_dev = frame_keys.shape[0]
    key_part = lax.all_gather(frame_keys, ("frm", "pos"), axis=0, tiled=True)
    value_part = lax.all_gather(frame_values, ("frm", "pos"), axis=0, tiled=True)
    row_count = key_part.shape[0]
    row_ids = jnp.arange(row_count, dtype=jnp.int32)
    frame_ids = (
        row_ids // rows_dev // pos_count * frames_dev + row_ids % rows_dev // half_tokens * KSTRIDE
    )
    allowed = (frame_ids[None, :] % strides[:, None] == 0)[:, None, :]
    scores = (
        jnp.einsum("qhd,khd->hqk", query_rows, key_part, precision=lax.Precision.HIGHEST)
        * score_scale
    )
    top_old = jnp.full((heads_local, query_count), -1e30, jnp.float32)
    top_new = jnp.maximum(top_old, jnp.max(jnp.where(allowed, scores, -1e30), axis=2))
    weights = jnp.where(allowed, jnp.exp(scores - top_new[:, :, None]), 0.0)
    total_new = jnp.sum(weights, axis=2)
    accum_new = jnp.einsum("hqk,khd->hqd", weights, value_part, precision=lax.Precision.HIGHEST)
    final_state = (top_new, total_new, accum_new)
    _, total_final, accum_final = final_state
    global_out = jnp.transpose(accum_final / total_final[:, :, None], (1, 0, 2))
    frequency = jnp.arange(total_frames, dtype=jnp.int32)
    phase_index = frequency[:, None] * frequency[None, :] % total_frames
    phases = 2.0 * math.pi / total_frames * phase_index.astype(jnp.float32)
    cos_table = jnp.cos(phases)
    sin_table = jnp.sin(phases)
    distance_freq = jnp.minimum(frequency, total_frames - frequency)
    low_keep = (distance_freq[None, :] <= cutoffs[:, None]).astype(jnp.float32)
    lowpass = (
        jnp.einsum("kf,hk,kg->hfg", cos_table, low_keep, cos_table, precision=lax.Precision.HIGHEST)
        + jnp.einsum(
            "kf,hk,kg->hfg", sin_table, low_keep, sin_table, precision=lax.Precision.HIGHEST
        )
    ) / total_frames
    group_items = half_tokens // frame_groups
    local_grid = local_out.reshape(frames_dev, frame_groups, group_items, channels)
    global_grid = global_out.reshape(frames_dev, frame_groups, group_items, channels)
    frame_block = lax.all_to_all(
        global_grid - local_grid, "frm", split_axis=1, concat_axis=0, tiled=True
    )
    frames_all = frame_block.shape[0]
    item_count = frame_block.shape[2]
    shaped = frame_block.reshape(frames_all, item_count, heads_local, DH)
    filtered_block = jnp.einsum(
        "hfg,gihd->fihd", lowpass, shaped, precision=lax.Precision.HIGHEST
    ).reshape(frame_block.shape)
    filtered = lax.all_to_all(filtered_block, "frm", split_axis=0, concat_axis=1, tiled=True)
    blended = local_grid + filtered
    return blended.reshape(frames_dev, half_tokens, channels)


def splits_by_heads(heads_local, parts, pos_count):
    return heads_local % parts == 0 and pos_count == 2 and parts.bit_count() == 1


def shards(queries, key_states, value_states, windows, strides, cutoffs):
    heads_local = queries.shape[2] // DH
    if splits_by_heads(heads_local, lax.axis_size("frm"), lax.axis_size("pos")):
        return by_heads(queries, key_states, value_states, windows, strides, cutoffs)
    return by_frames(queries, key_states, value_states, windows, strides, cutoffs)


def solution(mesh):
    in_specs = (
        P(("grp", "frm"), "pos", "head"),
        P(("grp", "frm"), "pos", "head"),
        P(("grp", "frm"), "pos", "head"),
        P("head"),
        P("head"),
        P("head"),
    )
    out_specs = P(("grp", "frm"), "pos", "head")
    return jax.shard_map(
        shards, mesh=mesh, in_specs=in_specs, out_specs=out_specs, check_vma=False
    )
```

```python
import functools
import math

import jax
import jax.numpy as jnp
import numpy as np
from jax import lax
from jax.experimental import pallas as pl
from jax.experimental.pallas import tpu as pltpu
from jax.sharding import PartitionSpec as P


DH = 128
KSTRIDE = 4
WMAX = 2
MASKED = -1e30
GROUP = 4
HALF_GROUP = 2
ATTEND_VMEM = 24 * 2**20
BLEND = 8


def lowpass_table(frames):
    cutoff = np.arange(frames // 2 + 1)
    freq = np.arange(frames)
    keep = (np.minimum(freq, frames - freq)[None, :] <= cutoff[:, None]).astype(np.float64)
    waves = np.cos(2.0 * np.pi / frames * (np.outer(freq, freq) % frames))
    return (keep @ waves / frames).astype(np.float32)


def wires(parts):
    return sorted(range(1, parts), key=lambda hop: (hop.bit_count() % 2 == 0, -hop))


def pack_kernel(slot, parts, per_part, *refs):
    sources, outs = refs[:3], refs[3 : 3 + parts]
    held, load_sem, store_sem = refs[3 + parts :]
    me = lax.axis_index("frm")
    order = [*wires(parts), 0]
    loads, stores = {}, {}
    for hop in order:
        owner = lax.bitwise_xor(me, hop)
        columns = pl.ds(pl.multiple_of((owner * per_part + slot) * DH, DH), DH)
        for at in range(3):
            loads[hop, at] = pltpu.make_async_copy(
                sources[at].at[:, :, columns], held.at[hop, at], load_sem.at[hop, at]
            )
            loads[hop, at].start()
    for hop in order:
        for at in range(3):
            loads[hop, at].wait()
        stores[hop] = pltpu.make_async_copy(held.at[hop], outs[hop], store_sem.at[hop])
        stores[hop].start()
    for hop in order:
        stores[hop].wait()


def pack(slot, parts, queries, key_states, value_states, per_part):
    frames_dev, rows, _ = queries.shape
    piece = (3, frames_dev, rows, DH)
    moved = parts * math.prod(piece) * 4
    return pl.pallas_call(
        functools.partial(pack_kernel, slot, parts, per_part),
        out_shape=[jax.ShapeDtypeStruct(piece, jnp.float32)] * parts,
        in_specs=[pl.BlockSpec(memory_space=pl.ANY)] * 3,
        out_specs=[pl.BlockSpec(memory_space=pl.ANY)] * parts,
        scratch_shapes=[
            pltpu.VMEM((parts, *piece), jnp.float32),
            pltpu.SemaphoreType.DMA((parts, 3)),
            pltpu.SemaphoreType.DMA((parts,)),
        ],
        cost_estimate=pl.CostEstimate(flops=0, bytes_accessed=2 * moved, transcendentals=0),
    )(queries, key_states, value_states)


def split(value):
    high = value.astype(jnp.bfloat16)
    return high, (value - high.astype(jnp.float32)).astype(jnp.bfloat16)


def attend_kernel(slot, parts, per_part, riders, *refs):
    windows, strides, cutoffs, table = refs[:4]
    refs = refs[4:]
    mine, theirs, refs = refs[:parts], refs[parts : 2 * parts], refs[2 * parts :]
    earlier, refs = (refs[:parts], refs[parts:]) if riders else ((), refs)
    outs, refs = refs[:parts], refs[parts:]
    (q_in, k_in, v_in, q_cat, k_cat, v_cat, kg_cat, vg_cat, local, diff, load_sem, store_sem) = refs[
        :12
    ]
    frames, rows, _ = q_in.shape
    tokens = k_in.shape[1]
    frames_dev = frames // parts
    me = lax.axis_index("frm")
    head = me * per_part + slot
    window, stride, cutoff = windows[head], strides[head], cutoffs[head]

    loads = []
    for hop in range(parts):
        owner = lax.bitwise_xor(me, hop)
        span = pl.ds(owner * frames_dev, frames_dev)
        near, far = pl.ds(0, rows), pl.ds(rows, rows)
        loads.append([])
        for at, (source, target) in enumerate(
            (
                (mine[hop].at[0], q_in.at[span]),
                (mine[hop].at[1], k_in.at[span, near]),
                (theirs[hop].at[1], k_in.at[span, far]),
                (mine[hop].at[2], v_in.at[span, near]),
                (theirs[hop].at[2], v_in.at[span, far]),
            )
        ):
            copy = pltpu.make_async_copy(source, target, load_sem.at[hop, at])
            copy.start()
            loads[-1].append(copy)

    if riders:
        held, ride_sem = refs[12:]
        rides = [
            pltpu.make_async_copy(earlier[hop], held.at[hop], ride_sem.at[0, hop])
            for hop in range(parts)
        ]
        for copy in rides:
            copy.start()

    score_scale = DH ** (-0.5) * math.log2(math.e)

    def prepare(frame, carry):
        q_at = pl.ds(pl.multiple_of(frame * rows, rows), rows)
        k_at = pl.ds(pl.multiple_of(frame * tokens, tokens), tokens)
        high, low = split(q_in[frame] * score_scale)
        q_cat[q_at, 0:DH] = high
        q_cat[q_at, DH : 2 * DH] = low
        q_cat[q_at, 2 * DH : 3 * DH] = high
        k_high, k_low = split(k_in[frame])
        k_cat[k_at, 0:DH] = k_high
        k_cat[k_at, DH : 2 * DH] = k_high
        k_cat[k_at, 2 * DH : 3 * DH] = k_low
        v_high, v_low = split(v_in[frame].T)
        v_cat[0:DH, k_at] = v_high
        v_cat[DH : 2 * DH, k_at] = v_low
        return carry

    for hop in range(parts):
        owner = lax.bitwise_xor(me, hop)
        for copy in loads[hop]:
            copy.wait()
        lax.fori_loop(owner * frames_dev, (owner + 1) * frames_dev, prepare, 0)
    key_frames = frames // KSTRIDE
    for at in range(key_frames):
        source = pl.ds(at * KSTRIDE * tokens, tokens)
        target = pl.ds(at * tokens, tokens)
        kg_cat[target, :] = k_cat[source, :]
        vg_cat[:, target] = v_cat[:, source]

    group = GROUP
    reach = min(2 * WMAX + group, frames)
    group_rows = group * rows
    lane_frame = lax.broadcasted_iota(jnp.int32, (1, group_rows), 1) // rows

    def weighted(key_rows, bias, value_columns, query_rows):
        scores = lax.dot_general(
            key_rows, query_rows, (((1,), (1,)), ((), ())), preferred_element_type=jnp.float32
        )
        parts_of = [scores[at * tokens : (at + 1) * tokens] for at in range(len(bias))]
        peaks = [
            jnp.max(part, axis=0, keepdims=True) + shift for part, shift in zip(parts_of, bias)
        ]
        highest = functools.reduce(jnp.maximum, peaks)
        weights = jnp.concatenate(
            [jnp.exp2(part - (highest - shift)) for part, shift in zip(parts_of, bias)], axis=0
        )
        total = jnp.sum(weights, axis=0, keepdims=True)
        high, low = split(weights)
        wide = jnp.dot(value_columns, high, preferred_element_type=jnp.float32)
        rest = jnp.dot(value_columns[:DH], low, preferred_element_type=jnp.float32)
        return (wide[:DH] + wide[DH:] + rest) / total

    global_bias = [
        jnp.where(lax.rem(at * KSTRIDE, stride) == 0, 0.0, MASKED) for at in range(key_frames)
    ]

    def per_group(step, carry):
        first = step * group
        start = jnp.clip(first - WMAX, 0, frames - reach)
        q_part = q_cat[pl.ds(pl.multiple_of(first * rows, group_rows), group_rows), :]
        k_at = pl.ds(pl.multiple_of(start * tokens, tokens), reach * tokens)
        local_bias = [
            jnp.where(jnp.abs(start + at - first - lane_frame) <= window, 0.0, MASKED)
            for at in range(reach)
        ]
        local_part = weighted(k_cat[k_at, :], local_bias, v_cat[:, k_at], q_part)
        global_part = weighted(kg_cat[...], global_bias, vg_cat[...], q_part)
        difference = (global_part - local_part).T
        local_part = local_part.T
        for at in range(group):
            local[first + at] = local_part[at * rows : (at + 1) * rows]
            diff[first + at] = difference[at * rows : (at + 1) * rows]
        return carry

    lax.fori_loop(0, frames // group, per_group, 0)

    stores = []
    for hop in range(parts if riders else 0):
        rides[hop].wait()
        stores.append(
            pltpu.make_async_copy(held.at[hop], outs[hop].at[0:riders], ride_sem.at[1, hop])
        )
        stores[-1].start()

    half = frames // 2
    kept = jnp.clip(cutoff, 0, half)
    even = [0.5 * (table[kept, at] + table[kept, at + half]) for at in range(half)]
    odd = [0.5 * (table[kept, at] - table[kept, at + half]) for at in range(half)]

    def blend(row, carry):
        at = pl.ds(pl.multiple_of(row * BLEND, BLEND), BLEND)
        first = [diff[frame, at] for frame in range(half)]
        second = [diff[frame + half, at] for frame in range(half)]
        sums = [x + y for x, y in zip(first, second)]
        gaps = [x - y for x, y in zip(first, second)]
        for frame in range(half):
            periodic = sum(even[(frame - other) % half] * sums[other] for other in range(half))
            turning = sum(
                (odd[frame - other] if other <= frame else -odd[frame - other + half]) * gaps[other]
                for other in range(half)
            )
            q_in[frame, at] = local[frame, at] + (periodic + turning)
            q_in[frame + half, at] = local[frame + half, at] + (periodic - turning)
        return carry

    lax.fori_loop(0, rows // BLEND, blend, 0)
    for hop in range(parts):
        owner = lax.bitwise_xor(me, hop)
        stores.append(
            pltpu.make_async_copy(
                q_in.at[pl.ds(owner * frames_dev, frames_dev)], outs[hop].at[riders], store_sem.at[hop]
            )
        )
        stores[-1].start()
    for copy in stores:
        copy.wait()


def attend_head(slot, parts, scalars, table, mine, theirs, earlier, per_part):
    _, frames_dev, rows, _ = mine[0].shape
    frames, tokens = frames_dev * parts, 2 * rows
    key_frames = frames // KSTRIDE
    riders = earlier[0].shape[0] if earlier else 0
    result = (riders + 1, frames_dev, rows, DH)
    scratch = []
    if riders:
        scratch = [
            pltpu.VMEM((parts, riders, frames_dev, rows, DH), jnp.float32),
            pltpu.SemaphoreType.DMA((2, parts)),
        ]
    flops = 12 * frames * rows * (5 + key_frames) * tokens * DH
    return pl.pallas_call(
        functools.partial(attend_kernel, slot, parts, per_part, riders),
        out_shape=[jax.ShapeDtypeStruct(result, jnp.float32)] * parts,
        in_specs=[pl.BlockSpec(memory_space=pltpu.SMEM)] * 4
        + [pl.BlockSpec(memory_space=pl.ANY)] * (2 * parts + len(earlier)),
        out_specs=[pl.BlockSpec(memory_space=pl.ANY)] * parts,
        scratch_shapes=[
            pltpu.VMEM((frames, rows, DH), jnp.float32),
            pltpu.VMEM((frames, tokens, DH), jnp.float32),
            pltpu.VMEM((frames, tokens, DH), jnp.float32),
            pltpu.VMEM((frames * rows, 3 * DH), jnp.bfloat16),
            pltpu.VMEM((frames * tokens, 3 * DH), jnp.bfloat16),
            pltpu.VMEM((2 * DH, frames * tokens), jnp.bfloat16),
            pltpu.VMEM((key_frames * tokens, 3 * DH), jnp.bfloat16),
            pltpu.VMEM((2 * DH, key_frames * tokens), jnp.bfloat16),
            pltpu.VMEM((frames, rows, DH), jnp.float32),
            pltpu.VMEM((frames, rows, DH), jnp.float32),
            pltpu.SemaphoreType.DMA((parts, 5)),
            pltpu.SemaphoreType.DMA((parts,)),
        ]
        + scratch,
        cost_estimate=pl.CostEstimate(
            flops=flops,
            bytes_accessed=6 * frames * rows * DH * 4,
            transcendentals=frames * rows * (5 + key_frames) * tokens,
        ),
        compiler_params=pltpu.CompilerParams(vmem_limit_bytes=ATTEND_VMEM),
    )(*scalars, table, *mine, *theirs, *earlier)


def unpack_kernel(parts, per_part, first, *refs):
    pieces, refs = refs[:parts], refs[parts:]
    out, held, load_sem, store_sem = refs[-4:]
    slots = held.shape[1]
    me = lax.axis_index("frm")
    loads, stores = [], []
    for hop in range(parts):
        loads.append(pltpu.make_async_copy(pieces[hop], held.at[hop], load_sem.at[hop]))
        loads[-1].start()
    for hop in range(parts):
        owner = lax.bitwise_xor(me, hop)
        loads[hop].wait()
        for at in range(slots):
            columns = pl.ds(pl.multiple_of((owner * per_part + first + at) * DH, DH), DH)
            stores.append(
                pltpu.make_async_copy(held.at[hop, at], out.at[:, :, columns], store_sem.at[hop, at])
            )
            stores[-1].start()
    for copy in stores:
        copy.wait()


def unpack(parts, per_part, first, pieces, channels):
    slots, frames_dev, rows, _ = pieces[0].shape
    operands = list(pieces)
    return pl.pallas_call(
        functools.partial(unpack_kernel, parts, per_part, first),
        out_shape=jax.ShapeDtypeStruct((frames_dev, rows, channels), jnp.float32),
        in_specs=[pl.BlockSpec(memory_space=pl.ANY)] * len(operands),
        out_specs=pl.BlockSpec(memory_space=pl.ANY),
        scratch_shapes=[
            pltpu.VMEM((parts, slots, frames_dev, rows, DH), jnp.float32),
            pltpu.SemaphoreType.DMA((parts,)),
            pltpu.SemaphoreType.DMA((parts, slots)),
        ],
        name="unpack",
    )(*operands)


def swap_pack_kernel(slots, *refs):
    sources, out = refs[:3], refs[3]
    held, load_sem, store_sem = refs[4:]
    core = lax.axis_index("pos")
    loads = []
    for slot in range(slots):
        for side in range(2):
            columns = head_columns(slot, side, 1 - core)
            for kind in range(3):
                loads.append(
                    pltpu.make_async_copy(
                        sources[kind].at[:, :, columns],
                        held.at[slot, side, kind],
                        load_sem.at[slot, side, kind],
                    )
                )
                loads[-1].start()
    stores = []
    for slot in range(slots):
        for copy in loads[6 * slot : 6 * slot + 6]:
            copy.wait()
        stores.append(pltpu.make_async_copy(held.at[slot], out.at[slot], store_sem.at[slot]))
        stores[-1].start()
    for copy in stores:
        copy.wait()


def swap_pack(slots, queries, key_states, value_states):
    frames_dev, rows, _ = queries.shape
    piece = (slots, 2, 3, frames_dev, rows, DH)
    return pl.pallas_call(
        functools.partial(swap_pack_kernel, slots),
        out_shape=jax.ShapeDtypeStruct(piece, jnp.float32),
        in_specs=[pl.BlockSpec(memory_space=pl.ANY)] * 3,
        out_specs=pl.BlockSpec(memory_space=pl.ANY),
        scratch_shapes=[
            pltpu.VMEM(piece, jnp.float32),
            pltpu.SemaphoreType.DMA((slots, 2, 3)),
            pltpu.SemaphoreType.DMA((slots,)),
        ],
        name="swap_pack",
    )(queries, key_states, value_states)


def full_pack_kernel(slot, *refs):
    sources, swapped = refs[:3], refs[3]
    side_out, key_out, halo_out = refs[4], refs[5:7], refs[7:9]
    held, load_sem, store_sem = refs[9:]
    frames_dev, rows, _ = sources[0].shape
    me, core = lax.axis_index("frm"), lax.axis_index("pos")
    near_end = jnp.where(me < lax.axis_size("frm") // 2, frames_dev - WMAX, 1)
    near, far = pl.ds(0, rows), pl.ds(rows, rows)
    loads = []
    for at in (1, 0):
        side = lax.bitwise_xor(lax.rem(me, 2), at)
        columns = head_columns(slot, side, core)
        for kind in range(3) if at else range(1, 3):
            loads += [
                pltpu.make_async_copy(
                    sources[kind].at[:, :, columns], held.at[at, kind, :, near], load_sem.at[at, kind, 0]
                ),
                pltpu.make_async_copy(
                    swapped.at[slot, side, kind], held.at[at, kind, :, far], load_sem.at[at, kind, 1]
                ),
            ]
    for copy in loads:
        copy.start()
    stores = []
    for at, count in ((1, 6), (0, 4)):
        for copy in loads[:count]:
            copy.wait()
        loads = loads[count:]
        if at:
            stores.append(pltpu.make_async_copy(held.at[1], side_out, store_sem.at[0, 0]))
        stores += [
            pltpu.make_async_copy(
                held.at[at, 1:3, pl.ds(near_end, WMAX)], halo_out[at], store_sem.at[1, at]
            ),
            pltpu.make_async_copy(held.at[at, 1:3, 0:1], key_out[at], store_sem.at[2, at]),
        ]
        for copy in stores[-3 if at else -2 :]:
            copy.start()
    for copy in stores:
        copy.wait()


def full_pack(slot, queries, key_states, value_states, swapped):
    frames_dev, rows, _ = queries.shape
    tokens = 2 * rows
    side, key, halo = ((3, frames_dev), (2, 1), (2, WMAX))
    shapes = [side, key, key, halo, halo]
    outs = pl.pallas_call(
        functools.partial(full_pack_kernel, slot),
        out_shape=[jax.ShapeDtypeStruct((*x, tokens, DH), jnp.float32) for x in shapes],
        in_specs=[pl.BlockSpec(memory_space=pl.ANY)] * 4,
        out_specs=[pl.BlockSpec(memory_space=pl.ANY)] * 5,
        scratch_shapes=[
            pltpu.VMEM((2, 3, frames_dev, tokens, DH), jnp.float32),
            pltpu.SemaphoreType.DMA((2, 3, 2)),
            pltpu.SemaphoreType.DMA((3, 2)),
        ],
    )(queries, key_states, value_states, swapped)
    return outs[0], outs[1:3], outs[3:5]


def head_columns(slot, side, core):
    return pl.ds(pl.multiple_of((4 * slot + 2 * side + core) * DH, DH), DH)


def attention(key_rows, bias, value_columns, query_rows):
    scores = lax.dot_general(
        key_rows, query_rows, (((1,), (1,)), ((), ())), preferred_element_type=jnp.float32
    )
    tokens = scores.shape[0] // len(bias)
    blocks = [scores[at * tokens : (at + 1) * tokens] for at in range(len(bias))]
    peaks = [jnp.max(block, axis=0, keepdims=True) + shift for block, shift in zip(blocks, bias)]
    highest = functools.reduce(jnp.maximum, peaks)
    weights = jnp.concatenate(
        [jnp.exp2(block - (highest - shift)) for block, shift in zip(blocks, bias)], axis=0
    )
    total = jnp.sum(weights, axis=0, keepdims=True)
    high, low = split(weights)
    wide = jnp.dot(value_columns, high, preferred_element_type=jnp.float32)
    rest = jnp.dot(value_columns[:DH], low, preferred_element_type=jnp.float32)
    return (wide[:DH] + wide[DH:] + rest) / total


def waves(frames, top):
    angle = 2.0 * np.pi / frames * np.arange(frames // 2)
    rows = [np.ones(frames // 2)]
    for k in range(1, top + 1):
        rows += [np.cos(k * angle), np.sin(k * angle)]
    return [[float(x) for x in row] for row in rows]


def half_sign(row, half):
    return 1.0 - 2.0 * half.astype(jnp.float32) if (row + 1) // 2 % 2 else 1.0


def attend_half_kernel(slot, parts, top, *refs):
    windows, strides = refs[:2]
    sources, refs = refs[2:5], refs[5:]
    swapped, beside = refs[:2]
    keys, halos, refs = refs[2:4], refs[4:6], refs[6:]
    local_out, sums_out, refs = refs[0], refs[1], refs[2:]
    (q_in, k_in, v_in, kx_in, vx_in, q_cat, k_cat, v_cat, kg_cat, vg_cat, local, diff, sums) = refs[:13]
    load_sem, far_sem, store_sem = refs[13:]
    frames, tokens, _ = q_in.shape
    frames_dev, rows = frames // 2, tokens // 2
    me, core = lax.axis_index("frm"), lax.axis_index("pos")
    half, side = me // 2, lax.rem(me, 2)
    head = 4 * slot + 2 * side + core
    window, stride = windows[head], strides[head]
    columns = head_columns(slot, side, core)
    mine = pl.ds(side * frames_dev, frames_dev)
    others = pl.ds((1 - side) * frames_dev, frames_dev)
    near, far = pl.ds(0, rows), pl.ds(rows, rows)

    copies = []
    for at, target in enumerate((q_in, k_in, v_in)):
        copies += [
            pltpu.make_async_copy(sources[at].at[:, :, columns], target.at[mine, near], load_sem.at[at, 0]),
            pltpu.make_async_copy(
                swapped.at[slot, side, at], target.at[mine, far], load_sem.at[at, 1]
            ),
            pltpu.make_async_copy(beside.at[at], target.at[others], load_sem.at[at, 2]),
        ]
    for kind, target in enumerate((kx_in, vx_in)):
        for at in range(2):
            copies.append(
                pltpu.make_async_copy(
                    keys[at].at[kind], target.at[pl.ds(at, 1)], far_sem.at[0, kind, at]
                )
            )
    for copy in copies:
        copy.start()
    inner = (me > 0) & (me < parts - 1)

    def halo_copies(source):
        return [
            pltpu.make_async_copy(
                halos[source].at[kind], target.at[pl.ds(2, WMAX)], far_sem.at[1, kind, 0]
            )
            for kind, target in enumerate((kx_in, vx_in))
        ]

    for taken, first in ((inner, 1), (jnp.logical_not(inner), 0)):

        @pl.when(taken)
        def _(first=first):
            for copy in halo_copies(first):
                copy.start()
            for copy in halo_copies(first):
                copy.wait()

    for copy in copies:
        copy.wait()

    score_scale = DH ** (-0.5) * math.log2(math.e)

    def place(keys_f32, values_f32, to_keys, to_values, block):
        at = pl.ds(pl.multiple_of(block * tokens, tokens), tokens)
        k_high, k_low = split(keys_f32)
        to_keys[at, 0:DH] = k_high
        to_keys[at, DH : 2 * DH] = k_high
        to_keys[at, 2 * DH : 3 * DH] = k_low
        v_high, v_low = split(values_f32.T)
        to_values[0:DH, at] = v_high
        to_values[DH : 2 * DH, at] = v_low

    def prepare(frame, carry):
        at = pl.ds(pl.multiple_of(frame * tokens, tokens), tokens)
        high, low = split(q_in[frame] * score_scale)
        q_cat[at, 0:DH] = high
        q_cat[at, DH : 2 * DH] = low
        q_cat[at, 2 * DH : 3 * DH] = high
        place(k_in[frame], v_in[frame], k_cat, v_cat, frame + WMAX)
        return carry

    lax.fori_loop(0, frames, prepare, 0)
    edge = jnp.where(half == 0, frames + WMAX, 0)
    edge_from = (jnp.where(half == 0, side, 2), jnp.where(half == 0, 2, 3))
    for at in range(WMAX):
        place(kx_in[edge_from[at]], vx_in[edge_from[at]], k_cat, v_cat, edge + at)
    key_frame = [frames * half, frames * half + frames_dev]
    for at in range(2):
        source, target = pl.ds((WMAX + at * frames_dev) * tokens, tokens), pl.ds(at * tokens, tokens)
        kg_cat[target, :] = k_cat[source, :]
        vg_cat[:, target] = v_cat[:, source]
        place(kx_in[at], vx_in[at], kg_cat, vg_cat, 2 + at)
        key_frame.append(lax.bitwise_xor(me, 2 + at) * frames_dev)
    global_bias = [jnp.where(lax.rem(frame, stride) == 0, 0.0, MASKED) for frame in key_frame]

    group = HALF_GROUP
    reach = 2 * WMAX + group
    group_rows = group * tokens
    lane_frame = lax.broadcasted_iota(jnp.int32, (1, group_rows), 1) // tokens
    lowest = WMAX * (1 - half)

    def per_group(step, carry):
        first = step * group + WMAX
        start = jnp.clip(first - WMAX, lowest, lowest + frames + WMAX - reach)
        q_part = q_cat[pl.ds(pl.multiple_of(step * group_rows, group_rows), group_rows), :]
        k_at = pl.ds(pl.multiple_of(start * tokens, tokens), reach * tokens)
        local_bias = [
            jnp.where(jnp.abs(start + at - first - lane_frame) <= window, 0.0, MASKED)
            for at in range(reach)
        ]
        local_part = attention(k_cat[k_at, :], local_bias, v_cat[:, k_at], q_part)
        global_part = attention(kg_cat[...], global_bias, vg_cat[...], q_part)
        difference = (global_part - local_part).T
        local_part = local_part.T
        for at in range(group):
            local[step * group + at] = local_part[at * tokens : (at + 1) * tokens]
            diff[step * group + at] = difference[at * tokens : (at + 1) * tokens]
        return carry

    lax.fori_loop(0, frames // group, per_group, 0)
    to_local = pltpu.make_async_copy(local, local_out, store_sem.at[0])
    to_local.start()
    table = waves(2 * frames, top)

    def gather(row, carry):
        at = pl.ds(pl.multiple_of(row * BLEND, BLEND), BLEND)
        parts_of = [diff[frame, at] for frame in range(frames)]
        for wave, values in enumerate(table):
            total = sum(value * part for value, part in zip(values, parts_of))
            sums[wave, at] = total * half_sign(wave, half)
        return carry

    lax.fori_loop(0, tokens // BLEND, gather, 0)
    to_sums = pltpu.make_async_copy(sums, sums_out, store_sem.at[1])
    to_sums.start()
    to_local.wait()
    to_sums.wait()


def attend_half(slot, parts, top, scalars, sources, swapped, beside, keys, halos):
    frames_dev, rows, _ = sources[0].shape
    frames, tokens = 2 * frames_dev, 2 * rows
    waves_count = 2 * top + 1
    f32, bf16 = jnp.float32, jnp.bfloat16
    return pl.pallas_call(
        functools.partial(attend_half_kernel, slot, parts, top),
        out_shape=[
            jax.ShapeDtypeStruct((frames, tokens, DH), f32),
            jax.ShapeDtypeStruct((waves_count, tokens, DH), f32),
        ],
        in_specs=[pl.BlockSpec(memory_space=pltpu.SMEM)] * 2
        + [pl.BlockSpec(memory_space=pl.ANY)] * 9,
        out_specs=[pl.BlockSpec(memory_space=pl.ANY)] * 2,
        scratch_shapes=[pltpu.VMEM((frames, tokens, DH), f32)] * 3
        + [pltpu.VMEM((4, tokens, DH), f32)] * 2
        + [
            pltpu.VMEM((frames * tokens, 3 * DH), bf16),
            pltpu.VMEM(((frames + 2 * WMAX) * tokens, 3 * DH), bf16),
            pltpu.VMEM((2 * DH, (frames + 2 * WMAX) * tokens), bf16),
            pltpu.VMEM((4 * tokens, 3 * DH), bf16),
            pltpu.VMEM((2 * DH, 4 * tokens), bf16),
            pltpu.VMEM((frames, tokens, DH), f32),
            pltpu.VMEM((frames, tokens, DH), f32),
            pltpu.VMEM((waves_count, tokens, DH), f32),
            pltpu.SemaphoreType.DMA((3, 3)),
            pltpu.SemaphoreType.DMA((2, 2, 2)),
            pltpu.SemaphoreType.DMA((2,)),
        ],
        cost_estimate=pl.CostEstimate(
            flops=12 * frames * tokens * 10 * tokens * DH,
            bytes_accessed=6 * frames * tokens * DH * 4,
            transcendentals=frames * tokens * 10 * tokens,
        ),
        compiler_params=pltpu.CompilerParams(vmem_limit_bytes=ATTEND_VMEM),
    )(*scalars[:2], *sources, swapped, beside, *keys, *halos)


def mix_kernel(first, slots, top, *refs):
    cutoffs, refs = refs[0], refs[1:]
    outs, scratch = refs[3 * slots : 3 * slots + 4], refs[3 * slots + 4 :]
    local, own, other, load_sem, store_sem = scratch
    _, frames, tokens, _ = local.shape
    frames_dev, rows = frames // 2, tokens // 2
    me, core = lax.axis_index("frm"), lax.axis_index("pos")
    half, side = me // 2, lax.rem(me, 2)
    copies = [
        [
            pltpu.make_async_copy(refs[slots * at + slot], target.at[slot], load_sem.at[slot, at])
            for at, target in enumerate((own, other, local))
        ]
        for slot in range(slots)
    ]
    for copy in sum(copies, []):
        copy.start()
    table = waves(2 * frames, top)
    mine = pl.ds(side * frames_dev, frames_dev)
    others = pl.ds((1 - side) * frames_dev, frames_dev)
    near, far = pl.ds(0, rows), pl.ds(rows, rows)
    stores = []
    for slot in range(slots):
        cutoff = cutoffs[4 * (first + slot) + 2 * side + core]
        scales = []
        for wave in range(len(table)):
            k = (wave + 1) // 2
            share = (1.0 if k == 0 else 2.0) / (2 * frames)
            scales.append(jnp.where(cutoff >= k, share, 0.0) * half_sign(wave, half))
        for copy in copies[slot]:
            copy.wait()

        def blend(row, carry, slot=slot, scales=scales):
            at = pl.ds(pl.multiple_of(row * BLEND, BLEND), BLEND)
            parts_of = [
                scale * (own[slot, wave, at] + other[slot, wave, at])
                for wave, scale in enumerate(scales)
            ]
            for frame in range(frames):
                local[slot, frame, at] += sum(
                    values[frame] * part for values, part in zip(table, parts_of)
                )
            return carry

        lax.fori_loop(0, tokens // BLEND, blend, 0)
        for at, span in enumerate(((others, near), (others, far), (mine, far), (mine, near))):
            stores.append(
                pltpu.make_async_copy(
                    local.at[slot, *span], outs[at].at[slot], store_sem.at[slot, at]
                )
            )
            stores[-1].start()
    for copy in stores:
        copy.wait()


def mix(first, top, cutoffs, halves, passed):
    slots = len(halves)
    frames, tokens, _ = halves[0][0].shape
    sums = passed[0].shape
    piece = (slots, frames // 2, tokens // 2, DH)
    return pl.pallas_call(
        functools.partial(mix_kernel, first, slots, top),
        out_shape=[jax.ShapeDtypeStruct(piece, jnp.float32)] * 4,
        in_specs=[pl.BlockSpec(memory_space=pltpu.SMEM)]
        + [pl.BlockSpec(memory_space=pl.ANY)] * (3 * slots),
        out_specs=[pl.BlockSpec(memory_space=pl.ANY)] * 4,
        scratch_shapes=[
            pltpu.VMEM((slots, frames, tokens, DH), jnp.float32),
            pltpu.VMEM((slots, *sums), jnp.float32),
            pltpu.VMEM((slots, *sums), jnp.float32),
            pltpu.SemaphoreType.DMA((slots, 3)),
            pltpu.SemaphoreType.DMA((slots, 4)),
        ],
    )(cutoffs, *[x[1] for x in halves], *passed, *[x[0] for x in halves])


def half_unpack_kernel(first, *refs):
    pieces, refs = refs[:4], refs[4:]
    out, held, load_sem, store_sem = refs[-4:]
    slots = held.shape[1]
    me, core = lax.axis_index("frm"), lax.axis_index("pos")
    flips = ((1, 0), (1, 1), (0, 1), (0, 0))
    loads, stores = [], []
    for at in range(4):
        loads.append(pltpu.make_async_copy(pieces[at], held.at[at], load_sem.at[at]))
        loads[-1].start()
    for at, (side, flip) in enumerate(flips):
        loads[at].wait()
        for slot in range(slots):
            columns = head_columns(
                first + slot, lax.bitwise_xor(lax.rem(me, 2), side), lax.bitwise_xor(core, flip)
            )
            stores.append(
                pltpu.make_async_copy(
                    held.at[at, slot], out.at[:, :, columns], store_sem.at[at, slot]
                )
            )
            stores[-1].start()
    for copy in stores:
        copy.wait()


def half_unpack(first, pieces, out):
    slots, frames_dev, rows, _ = pieces[0].shape
    return pl.pallas_call(
        functools.partial(half_unpack_kernel, first),
        out_shape=jax.ShapeDtypeStruct(out.shape, jnp.float32),
        in_specs=[pl.BlockSpec(memory_space=pl.ANY)] * 5,
        out_specs=pl.BlockSpec(memory_space=pl.ANY),
        scratch_shapes=[
            pltpu.VMEM((4, slots, frames_dev, rows, DH), jnp.float32),
            pltpu.SemaphoreType.DMA((4,)),
            pltpu.SemaphoreType.DMA((4, slots)),
        ],
        input_output_aliases={4: 0},
    )(*pieces, out)


def across(value, hop, flip, chips=None):
    chips = range(lax.axis_size("frm")) if chips is None else chips
    pairs = [(2 * z + c, 2 * (z ^ hop) + (c ^ flip)) for z in chips for c in range(2)]
    return lax.ppermute(value, ("frm", "pos"), pairs)


def by_halves(queries, key_states, value_states, windows, strides, cutoffs):
    parts = lax.axis_size("frm")
    frames_dev, _, channels = queries.shape
    slots = channels // DH // 4 - 1
    frames = frames_dev * parts
    top = frames // 8
    table = jnp.asarray(lowpass_table(frames))
    scalars, sources = (windows, strides, cutoffs), (queries, key_states, value_states)
    inner = (parts // 2 - 1, parts // 2)
    packed = pack(4 * slots, parts, *sources, 1)
    packed, sources = lax.optimization_barrier((packed, sources))
    mine = [packed[0]] + [None] * (parts - 1)
    for hop in wires(parts):
        mine[hop] = around(packed[hop], hop)
    swapped = across(swap_pack(slots, *sources), 0, 1)
    beside, far_keys, far_halos = [], [], []
    for slot in range(slots):
        side, keys, halos = full_pack(slot, *sources, swapped)
        far_keys.append([])
        far_halos.append([])
        for at in range(2):
            far_halos[-1].append(across(halos[at], 2 + at, 0, inner))
            far_keys[-1].append(across(keys[at], 2 + at, 0))
        beside.append(across(side, 1, 0))
    theirs = []
    for hop in range(parts):
        theirs.append(swap(mine[hop]))
    done = attend_head(4 * slots, parts, scalars, table, mine, theirs, (), 1)
    landed = [done[0]] + [None] * (parts - 1)
    for hop in wires(parts):
        landed[hop] = around(done[hop], hop)
    pieces = []
    for slot in range(slots):
        half = attend_half(
            slot, parts, top, scalars, sources, swapped, beside[slot], far_keys[slot], far_halos[slot]
        )
        passed = across(half[1], 2, 0)
        mixed = mix(slot, top, cutoffs, [half], [passed])
        near = across(mixed[0], 1, 0)
        far = across(mixed[1], 1, 1)
        other = across(mixed[2], 0, 1)
        pieces.append([near, far, other, mixed[3]])
    out = unpack(parts, 1, 4 * slots, landed, channels)
    for slot in range(slots):
        out = half_unpack(slot, pieces[slot], out)
    return out


def around(value, hop):
    size = lax.axis_size("frm")
    return lax.ppermute(value, "frm", [(i, i ^ hop) for i in range(size)])


def swap(value):
    size = lax.axis_size("pos")
    return lax.ppermute(value, "pos", [(i, size - 1 - i) for i in range(size)])


def with_halo(value, sides, width):
    for axis, dim in sides:
        size, length = (lax.axis_size(axis), value.shape[dim])
        up = [(i, (i + 1) % size) for i in range(size - 1)]
        down = [(j, i) for i, j in up]
        last = lax.slice_in_dim(value, length - width, length, axis=dim)
        first = lax.slice_in_dim(value, 0, width, axis=dim)
        before = lax.ppermute(last, axis, up)
        after = lax.ppermute(first, axis, down)
        value = jnp.concatenate([before, value, after], axis=dim)
    return value


def attend(query_rows, key_rows, value_rows, allowed, score_scale):
    scores = (
        jnp.einsum("qhd,khd->hqk", query_rows, key_rows, precision=lax.Precision.HIGHEST)
        * score_scale
    )
    highest = jnp.max(jnp.where(allowed, scores, -1e30), axis=2, keepdims=True)
    weights = jnp.where(allowed, jnp.exp(scores - highest), 0.0)
    row_total = jnp.sum(weights, axis=2, keepdims=True)
    return jnp.einsum(
        "hqk,khd->qhd", weights / row_total, value_rows, precision=lax.Precision.HIGHEST
    )


def by_frames(queries, key_states, value_states, windows, strides, cutoffs):
    frames_dev, half_tokens, channels = queries.shape
    heads_local = channels // DH
    frame_groups = lax.axis_size("frm")
    pos_count = lax.axis_size("pos")
    total_frames = frames_dev * frame_groups
    halo_frames = frames_dev // 2
    score_scale = DH ** (-0.5)
    query_count = frames_dev * half_tokens
    query_rows = queries.reshape(query_count, heads_local, DH)
    query_blocks = queries.reshape(frames_dev, half_tokens, heads_local, DH)
    first_frame = lax.axis_index("frm") * frames_dev
    key_full, value_full = (
        lax.all_gather(key_states, "pos", axis=1, tiled=True),
        lax.all_gather(value_states, "pos", axis=1, tiled=True),
    )
    full_tokens = key_full.shape[1]
    stacked = jnp.stack([key_full, value_full])
    padded = with_halo(stacked, (("frm", 1),), halo_frames)
    window_span = 2 * halo_frames + 1
    span_rows = window_span * full_tokens
    span_offsets = jnp.arange(span_rows, dtype=jnp.int32) // full_tokens - halo_frames

    def local_frame(frame_local):
        query_part = lax.dynamic_index_in_dim(query_blocks, frame_local, 0, keepdims=False)
        block = lax.dynamic_slice_in_dim(padded, frame_local, window_span, 1)
        near_keys = block[0].reshape(span_rows, heads_local, DH)
        near_values = block[1].reshape(span_rows, heads_local, DH)
        near_frames = first_frame + frame_local + span_offsets
        inside = (near_frames >= 0) & (near_frames < total_frames)
        allowed = inside[None, None, :] & (
            jnp.abs(span_offsets)[None, None, :] <= windows[:, None, None]
        )
        return attend(query_part, near_keys, near_values, allowed, score_scale)

    local_out = lax.map(local_frame, jnp.arange(frames_dev, dtype=jnp.int32)).reshape(
        query_count, heads_local, DH
    )
    frame_keys = key_states[::KSTRIDE].reshape(-1, heads_local, DH)
    frame_values = value_states[::KSTRIDE].reshape(-1, heads_local, DH)
    rows_dev = frame_keys.shape[0]
    key_part = lax.all_gather(frame_keys, ("frm", "pos"), axis=0, tiled=True)
    value_part = lax.all_gather(frame_values, ("frm", "pos"), axis=0, tiled=True)
    row_count = key_part.shape[0]
    row_ids = jnp.arange(row_count, dtype=jnp.int32)
    frame_ids = (
        row_ids // rows_dev // pos_count * frames_dev + row_ids % rows_dev // half_tokens * KSTRIDE
    )
    allowed = (frame_ids[None, :] % strides[:, None] == 0)[:, None, :]
    scores = (
        jnp.einsum("qhd,khd->hqk", query_rows, key_part, precision=lax.Precision.HIGHEST)
        * score_scale
    )
    top_old = jnp.full((heads_local, query_count), -1e30, jnp.float32)
    top_new = jnp.maximum(top_old, jnp.max(jnp.where(allowed, scores, -1e30), axis=2))
    weights = jnp.where(allowed, jnp.exp(scores - top_new[:, :, None]), 0.0)
    total_new = jnp.sum(weights, axis=2)
    accum_new = jnp.einsum("hqk,khd->hqd", weights, value_part, precision=lax.Precision.HIGHEST)
    final_state = (top_new, total_new, accum_new)
    _, total_final, accum_final = final_state
    global_out = jnp.transpose(accum_final / total_final[:, :, None], (1, 0, 2))
    frequency = jnp.arange(total_frames, dtype=jnp.int32)
    phase_index = frequency[:, None] * frequency[None, :] % total_frames
    phases = 2.0 * math.pi / total_frames * phase_index.astype(jnp.float32)
    cos_table = jnp.cos(phases)
    sin_table = jnp.sin(phases)
    distance_freq = jnp.minimum(frequency, total_frames - frequency)
    low_keep = (distance_freq[None, :] <= cutoffs[:, None]).astype(jnp.float32)
    lowpass = (
        jnp.einsum("kf,hk,kg->hfg", cos_table, low_keep, cos_table, precision=lax.Precision.HIGHEST)
        + jnp.einsum(
            "kf,hk,kg->hfg", sin_table, low_keep, sin_table, precision=lax.Precision.HIGHEST
        )
    ) / total_frames
    group_items = half_tokens // frame_groups
    local_grid = local_out.reshape(frames_dev, frame_groups, group_items, channels)
    global_grid = global_out.reshape(frames_dev, frame_groups, group_items, channels)
    frame_block = lax.all_to_all(
        global_grid - local_grid, "frm", split_axis=1, concat_axis=0, tiled=True
    )
    frames_all = frame_block.shape[0]
    item_count = frame_block.shape[2]
    shaped = frame_block.reshape(frames_all, item_count, heads_local, DH)
    filtered_block = jnp.einsum(
        "hfg,gihd->fihd", lowpass, shaped, precision=lax.Precision.HIGHEST
    ).reshape(frame_block.shape)
    filtered = lax.all_to_all(filtered_block, "frm", split_axis=0, concat_axis=1, tiled=True)
    blended = local_grid + filtered
    return blended.reshape(frames_dev, half_tokens, channels)


def in_halves(heads_local, frames_dev, parts, pos_count):
    return heads_local % 4 == 0 and heads_local > 4 and frames_dev == KSTRIDE and (parts, pos_count) == (4, 2)


def shards(queries, key_states, value_states, windows, strides, cutoffs):
    heads_local = queries.shape[2] // DH
    if in_halves(heads_local, queries.shape[0], lax.axis_size("frm"), lax.axis_size("pos")):
        return by_halves(queries, key_states, value_states, windows, strides, cutoffs)
    return by_frames(queries, key_states, value_states, windows, strides, cutoffs)


def solution(mesh):
    in_specs = (
        P(("grp", "frm"), "pos", "head"),
        P(("grp", "frm"), "pos", "head"),
        P(("grp", "frm"), "pos", "head"),
        P("head"),
        P("head"),
        P("head"),
    )
    out_specs = P(("grp", "frm"), "pos", "head")
    return jax.shard_map(
        shards, mesh=mesh, in_specs=in_specs, out_specs=out_specs, check_vma=False
    )
```

```python
import functools
import math

import jax
import jax.numpy as jnp
import numpy as np
from jax import lax
from jax.experimental import pallas as pl
from jax.experimental.pallas import tpu as pltpu
from jax.sharding import PartitionSpec as P


DH = 128
KSTRIDE = 4
WMAX = 2
MASKED = -1e30
GROUP = 4
HALF_GROUP = 4
ATTEND_VMEM = 30 * 2**20
MOVE_VMEM = 10 * 2**20
FIRST_VMEM = 60 * 2**20
BLEND = 8


def lowpass_table(frames):
    cutoff = np.arange(frames // 2 + 1)
    freq = np.arange(frames)
    keep = (np.minimum(freq, frames - freq)[None, :] <= cutoff[:, None]).astype(np.float64)
    waves = np.cos(2.0 * np.pi / frames * (np.outer(freq, freq) % frames))
    return (keep @ waves / frames).astype(np.float32)


def wires(parts):
    return sorted(range(1, parts), key=lambda hop: (hop.bit_count() % 2 == 0, -hop))


def pack_kernel(slot, parts, per_part, *refs):
    sources, outs = refs[:3], refs[3 : 3 + parts]
    held, load_sem, store_sem = refs[3 + parts :]
    me = lax.axis_index("frm")
    order = [*wires(parts), 0]
    loads, stores = {}, {}
    for hop in order:
        owner = lax.bitwise_xor(me, hop)
        columns = pl.ds(pl.multiple_of((owner * per_part + slot) * DH, DH), DH)
        for at in range(3):
            loads[hop, at] = pltpu.make_async_copy(
                sources[at].at[:, :, columns], held.at[hop, at], load_sem.at[hop, at]
            )
            loads[hop, at].start()
    for hop in order:
        for at in range(3):
            loads[hop, at].wait()
        stores[hop] = pltpu.make_async_copy(held.at[hop], outs[hop], store_sem.at[hop])
        stores[hop].start()
    for hop in order:
        stores[hop].wait()


def pack(slot, parts, queries, key_states, value_states, per_part):
    frames_dev, rows, _ = queries.shape
    piece = (3, frames_dev, rows, DH)
    moved = parts * math.prod(piece) * 4
    return pl.pallas_call(
        functools.partial(pack_kernel, slot, parts, per_part),
        out_shape=[jax.ShapeDtypeStruct(piece, jnp.float32)] * parts,
        in_specs=[pl.BlockSpec(memory_space=pl.ANY)] * 3,
        out_specs=[pl.BlockSpec(memory_space=pl.ANY)] * parts,
        scratch_shapes=[
            pltpu.VMEM((parts, *piece), jnp.float32),
            pltpu.SemaphoreType.DMA((parts, 3)),
            pltpu.SemaphoreType.DMA((parts,)),
        ],
        cost_estimate=pl.CostEstimate(flops=0, bytes_accessed=2 * moved, transcendentals=0),
        compiler_params=pltpu.CompilerParams(vmem_limit_bytes=FIRST_VMEM),
    )(queries, key_states, value_states)


def split(value):
    high = value.astype(jnp.bfloat16)
    return high, (value - high.astype(jnp.float32)).astype(jnp.bfloat16)


def attend_kernel(slot, parts, per_part, *refs):
    windows, strides, cutoffs, table = refs[:4]
    refs = refs[4:]
    mine, theirs, refs = refs[:parts], refs[parts : 2 * parts], refs[2 * parts :]
    outs, refs = refs[:parts], refs[parts:]
    (q_in, k_in, v_in, q_cat, k_cat, v_cat, kg_cat, vg_cat, local, diff, load_sem, store_sem) = refs[
        :12
    ]
    frames, rows, _ = q_in.shape
    tokens = k_in.shape[1]
    frames_dev = frames // parts
    me = lax.axis_index("frm")
    head = me * per_part + slot
    window, stride, cutoff = windows[head], strides[head], cutoffs[head]

    loads = []
    for hop in range(parts):
        owner = lax.bitwise_xor(me, hop)
        span = pl.ds(owner * frames_dev, frames_dev)
        near, far = pl.ds(0, rows), pl.ds(rows, rows)
        loads.append([])
        for at, (source, target) in enumerate(
            (
                (mine[hop].at[0], q_in.at[span]),
                (mine[hop].at[1], k_in.at[span, near]),
                (theirs[hop].at[1], k_in.at[span, far]),
                (mine[hop].at[2], v_in.at[span, near]),
                (theirs[hop].at[2], v_in.at[span, far]),
            )
        ):
            copy = pltpu.make_async_copy(source, target, load_sem.at[hop, at])
            copy.start()
            loads[-1].append(copy)

    score_scale = DH ** (-0.5) * math.log2(math.e)

    def prepare(frame, carry):
        q_at = pl.ds(pl.multiple_of(frame * rows, rows), rows)
        k_at = pl.ds(pl.multiple_of(frame * tokens, tokens), tokens)
        high, low = split(q_in[frame] * score_scale)
        q_cat[q_at, 0:DH] = high
        q_cat[q_at, DH : 2 * DH] = low
        q_cat[q_at, 2 * DH : 3 * DH] = high
        k_high, k_low = split(k_in[frame])
        k_cat[k_at, 0:DH] = k_high
        k_cat[k_at, DH : 2 * DH] = k_high
        k_cat[k_at, 2 * DH : 3 * DH] = k_low
        v_high, v_low = split(v_in[frame].T)
        v_cat[0:DH, k_at] = v_high
        v_cat[DH : 2 * DH, k_at] = v_low
        return carry

    for hop in range(parts):
        owner = lax.bitwise_xor(me, hop)
        for copy in loads[hop]:
            copy.wait()
        lax.fori_loop(owner * frames_dev, (owner + 1) * frames_dev, prepare, 0)
    key_frames = frames // KSTRIDE
    for at in range(key_frames):
        source = pl.ds(at * KSTRIDE * tokens, tokens)
        target = pl.ds(at * tokens, tokens)
        kg_cat[target, :] = k_cat[source, :]
        vg_cat[:, target] = v_cat[:, source]

    group = GROUP
    reach = min(2 * WMAX + group, frames)
    group_rows = group * rows
    lane_frame = lax.broadcasted_iota(jnp.int32, (1, group_rows), 1) // rows

    def weighted(key_rows, bias, value_columns, query_rows):
        scores = lax.dot_general(
            key_rows, query_rows, (((1,), (1,)), ((), ())), preferred_element_type=jnp.float32
        )
        parts_of = [scores[at * tokens : (at + 1) * tokens] for at in range(len(bias))]
        peaks = [
            jnp.max(part, axis=0, keepdims=True) + shift for part, shift in zip(parts_of, bias)
        ]
        highest = functools.reduce(jnp.maximum, peaks)
        weights = jnp.concatenate(
            [jnp.exp2(part - (highest - shift)) for part, shift in zip(parts_of, bias)], axis=0
        )
        total = jnp.sum(weights, axis=0, keepdims=True)
        high, low = split(weights)
        wide = jnp.dot(value_columns, high, preferred_element_type=jnp.float32)
        rest = jnp.dot(value_columns[:DH], low, preferred_element_type=jnp.float32)
        return (wide[:DH] + wide[DH:] + rest) / total

    global_bias = [
        jnp.where(lax.rem(at * KSTRIDE, stride) == 0, 0.0, MASKED) for at in range(key_frames)
    ]

    def per_group(step, carry):
        first = step * group
        start = jnp.clip(first - WMAX, 0, frames - reach)
        q_part = q_cat[pl.ds(pl.multiple_of(first * rows, group_rows), group_rows), :]
        k_at = pl.ds(pl.multiple_of(start * tokens, tokens), reach * tokens)
        local_bias = [
            jnp.where(jnp.abs(start + at - first - lane_frame) <= window, 0.0, MASKED)
            for at in range(reach)
        ]
        local_part = weighted(k_cat[k_at, :], local_bias, v_cat[:, k_at], q_part)
        global_part = weighted(kg_cat[...], global_bias, vg_cat[...], q_part)
        difference = (global_part - local_part).T
        local_part = local_part.T
        for at in range(group):
            local[first + at] = local_part[at * rows : (at + 1) * rows]
            diff[first + at] = difference[at * rows : (at + 1) * rows]
        return carry

    lax.fori_loop(0, frames // group, per_group, 0)

    stores = []
    half = frames // 2
    kept = jnp.clip(cutoff, 0, half)
    even = [0.5 * (table[kept, at] + table[kept, at + half]) for at in range(half)]
    odd = [0.5 * (table[kept, at] - table[kept, at + half]) for at in range(half)]

    def blend(row, carry):
        at = pl.ds(pl.multiple_of(row * BLEND, BLEND), BLEND)
        first = [diff[frame, at] for frame in range(half)]
        second = [diff[frame + half, at] for frame in range(half)]
        sums = [x + y for x, y in zip(first, second)]
        gaps = [x - y for x, y in zip(first, second)]
        for frame in range(half):
            periodic = sum(even[(frame - other) % half] * sums[other] for other in range(half))
            turning = sum(
                (odd[frame - other] if other <= frame else -odd[frame - other + half]) * gaps[other]
                for other in range(half)
            )
            q_in[frame, at] = local[frame, at] + (periodic + turning)
            q_in[frame + half, at] = local[frame + half, at] + (periodic - turning)
        return carry

    lax.fori_loop(0, rows // BLEND, blend, 0)
    for hop in range(parts):
        owner = lax.bitwise_xor(me, hop)
        stores.append(
            pltpu.make_async_copy(
                q_in.at[pl.ds(owner * frames_dev, frames_dev)], outs[hop], store_sem.at[hop]
            )
        )
        stores[-1].start()
    for copy in stores:
        copy.wait()


def attend_head(slot, parts, scalars, table, mine, theirs, per_part):
    _, frames_dev, rows, _ = mine[0].shape
    frames, tokens = frames_dev * parts, 2 * rows
    key_frames = frames // KSTRIDE
    result = (frames_dev, rows, DH)
    flops = 12 * frames * rows * (5 + key_frames) * tokens * DH
    return pl.pallas_call(
        functools.partial(attend_kernel, slot, parts, per_part),
        out_shape=[jax.ShapeDtypeStruct(result, jnp.float32)] * parts,
        in_specs=[pl.BlockSpec(memory_space=pltpu.SMEM)] * 4
        + [pl.BlockSpec(memory_space=pl.ANY)] * (2 * parts),
        out_specs=[pl.BlockSpec(memory_space=pl.ANY)] * parts,
        scratch_shapes=[
            pltpu.VMEM((frames, rows, DH), jnp.float32),
            pltpu.VMEM((frames, tokens, DH), jnp.float32),
            pltpu.VMEM((frames, tokens, DH), jnp.float32),
            pltpu.VMEM((frames * rows, 3 * DH), jnp.bfloat16),
            pltpu.VMEM((frames * tokens, 3 * DH), jnp.bfloat16),
            pltpu.VMEM((2 * DH, frames * tokens), jnp.bfloat16),
            pltpu.VMEM((key_frames * tokens, 3 * DH), jnp.bfloat16),
            pltpu.VMEM((2 * DH, key_frames * tokens), jnp.bfloat16),
            pltpu.VMEM((frames, rows, DH), jnp.float32),
            pltpu.VMEM((frames, rows, DH), jnp.float32),
            pltpu.SemaphoreType.DMA((parts, 5)),
            pltpu.SemaphoreType.DMA((parts,)),
        ],
        cost_estimate=pl.CostEstimate(
            flops=flops,
            bytes_accessed=6 * frames * rows * DH * 4,
            transcendentals=frames * rows * (5 + key_frames) * tokens,
        ),
        compiler_params=pltpu.CompilerParams(vmem_limit_bytes=ATTEND_VMEM),
    )(*scalars, table, *mine, *theirs)


def unpack_kernel(slots, parts, *refs):
    count = parts + 4 * slots
    pieces, out, store_sem = refs[:count], refs[count], refs[count + 1]
    me, core = lax.axis_index("frm"), lax.axis_index("pos")
    stores = []
    for at in range(count):
        if at < parts:
            head = 4 * slots + lax.bitwise_xor(me, at)
            columns = pl.ds(pl.multiple_of(head * DH, DH), DH)
        else:
            slot, (side, flip) = (at - parts) // 4, ((1, 0), (1, 1), (0, 1), (0, 0))[(at - parts) % 4]
            columns = head_columns(
                slot, lax.bitwise_xor(lax.rem(me, 2), side), lax.bitwise_xor(core, flip)
            )
        stores.append(pltpu.make_async_copy(pieces[at], out.at[:, :, columns], store_sem.at[at]))
        stores[-1].start()
    for copy in stores:
        copy.wait()


def unpack(slots, parts, pieces, channels):
    frames_dev, rows, _ = pieces[0].shape
    count = len(pieces)
    return pl.pallas_call(
        functools.partial(unpack_kernel, slots, parts),
        out_shape=jax.ShapeDtypeStruct((frames_dev, rows, channels), jnp.float32),
        in_specs=[pl.BlockSpec(memory_space=pltpu.VMEM)] * count,
        out_specs=pl.BlockSpec(memory_space=pl.ANY),
        scratch_shapes=[pltpu.SemaphoreType.DMA((count,))],
        compiler_params=pltpu.CompilerParams(vmem_limit_bytes=MOVE_VMEM),
        name="unpack",
    )(*pieces)


def swap_pack_kernel(slots, *refs):
    sources, out = refs[:3], refs[3]
    held, load_sem, store_sem = refs[4:]
    core = lax.axis_index("pos")
    loads = []
    for slot in range(slots):
        for side in range(2):
            columns = head_columns(slot, side, 1 - core)
            for kind in range(3):
                loads.append(
                    pltpu.make_async_copy(
                        sources[kind].at[:, :, columns],
                        held.at[slot, side, kind],
                        load_sem.at[slot, side, kind],
                    )
                )
                loads[-1].start()
    stores = []
    for slot in range(slots):
        for copy in loads[6 * slot : 6 * slot + 6]:
            copy.wait()
        stores.append(pltpu.make_async_copy(held.at[slot], out.at[slot], store_sem.at[slot]))
        stores[-1].start()
    for copy in stores:
        copy.wait()


def swap_pack(slots, queries, key_states, value_states):
    frames_dev, rows, _ = queries.shape
    piece = (slots, 2, 3, frames_dev, rows, DH)
    return pl.pallas_call(
        functools.partial(swap_pack_kernel, slots),
        out_shape=jax.ShapeDtypeStruct(piece, jnp.float32),
        in_specs=[pl.BlockSpec(memory_space=pl.ANY)] * 3,
        out_specs=pl.BlockSpec(memory_space=pl.ANY),
        scratch_shapes=[
            pltpu.VMEM(piece, jnp.float32),
            pltpu.SemaphoreType.DMA((slots, 2, 3)),
            pltpu.SemaphoreType.DMA((slots,)),
        ],
        compiler_params=pltpu.CompilerParams(vmem_limit_bytes=FIRST_VMEM),
        name="swap_pack",
    )(queries, key_states, value_states)


def full_pack_kernel(slot, *refs):
    sources, swapped = refs[:3], refs[3]
    side_out, key_out, halo_out = refs[4], refs[5:7], refs[7:9]
    held, load_sem, store_sem = refs[9:]
    frames_dev, rows, _ = sources[0].shape
    me, core = lax.axis_index("frm"), lax.axis_index("pos")
    near_end = jnp.where(me < lax.axis_size("frm") // 2, frames_dev - WMAX, 1)
    near, far = pl.ds(0, rows), pl.ds(rows, rows)
    loads = []
    for at in (1, 0):
        side = lax.bitwise_xor(lax.rem(me, 2), at)
        columns = head_columns(slot, side, core)
        for kind in range(3) if at else range(1, 3):
            loads += [
                pltpu.make_async_copy(
                    sources[kind].at[:, :, columns], held.at[at, kind, :, near], load_sem.at[at, kind, 0]
                ),
                pltpu.make_async_copy(
                    swapped.at[slot, side, kind], held.at[at, kind, :, far], load_sem.at[at, kind, 1]
                ),
            ]
    for copy in loads:
        copy.start()
    stores = []
    for at, count in ((1, 6), (0, 4)):
        for copy in loads[:count]:
            copy.wait()
        loads = loads[count:]
        if at:
            stores.append(pltpu.make_async_copy(held.at[1], side_out, store_sem.at[0, 0]))
        stores += [
            pltpu.make_async_copy(
                held.at[at, 1:3, pl.ds(near_end, WMAX)], halo_out[at], store_sem.at[1, at]
            ),
            pltpu.make_async_copy(held.at[at, 1:3, 0:1], key_out[at], store_sem.at[2, at]),
        ]
        for copy in stores[-3 if at else -2 :]:
            copy.start()
    for copy in stores:
        copy.wait()


def full_pack(slot, queries, key_states, value_states, swapped):
    frames_dev, rows, _ = queries.shape
    tokens = 2 * rows
    side, key, halo = ((3, frames_dev), (2, 1), (2, WMAX))
    shapes = [side, key, key, halo, halo]
    outs = pl.pallas_call(
        functools.partial(full_pack_kernel, slot),
        out_shape=[jax.ShapeDtypeStruct((*x, tokens, DH), jnp.float32) for x in shapes],
        in_specs=[pl.BlockSpec(memory_space=pl.ANY)] * 4,
        out_specs=[pl.BlockSpec(memory_space=pl.ANY)] * 5,
        scratch_shapes=[
            pltpu.VMEM((2, 3, frames_dev, tokens, DH), jnp.float32),
            pltpu.SemaphoreType.DMA((2, 3, 2)),
            pltpu.SemaphoreType.DMA((3, 2)),
        ],
        compiler_params=pltpu.CompilerParams(vmem_limit_bytes=MOVE_VMEM),
    )(queries, key_states, value_states, swapped)
    return outs[0], outs[1:3], outs[3:5]


def head_columns(slot, side, core):
    return pl.ds(pl.multiple_of((4 * slot + 2 * side + core) * DH, DH), DH)


def attention(key_rows, bias, value_columns, query_rows):
    scores = lax.dot_general(
        key_rows, query_rows, (((1,), (1,)), ((), ())), preferred_element_type=jnp.float32
    )
    tokens = scores.shape[0] // len(bias)
    blocks = [scores[at * tokens : (at + 1) * tokens] for at in range(len(bias))]
    peaks = [jnp.max(block, axis=0, keepdims=True) + shift for block, shift in zip(blocks, bias)]
    highest = functools.reduce(jnp.maximum, peaks)
    weights = jnp.concatenate(
        [jnp.exp2(block - (highest - shift)) for block, shift in zip(blocks, bias)], axis=0
    )
    total = jnp.sum(weights, axis=0, keepdims=True)
    high, low = split(weights)
    wide = jnp.dot(value_columns, high, preferred_element_type=jnp.float32)
    rest = jnp.dot(value_columns[:DH], low, preferred_element_type=jnp.float32)
    return (wide[:DH] + wide[DH:] + rest) / total


def waves(frames, top):
    angle = 2.0 * np.pi / frames * np.arange(frames // 2)
    rows = [np.ones(frames // 2)]
    for k in range(1, top + 1):
        rows += [np.cos(k * angle), np.sin(k * angle)]
    return [[float(x) for x in row] for row in rows]


def half_sign(row, half):
    return 1.0 - 2.0 * half.astype(jnp.float32) if (row + 1) // 2 % 2 else 1.0


def attend_half_kernel(slot, parts, top, *refs):
    windows, strides = refs[:2]
    sources, refs = refs[2:5], refs[5:]
    swapped, beside = refs[:2]
    keys, halos, refs = refs[2:4], refs[4:6], refs[6:]
    local_out, sums_out, refs = refs[0], refs[1], refs[2:]
    (q_in, k_in, v_in, kx_in, vx_in, q_cat, k_cat, v_cat, kg_cat, vg_cat, local, diff, sums) = refs[:13]
    load_sem, far_sem, store_sem = refs[13:]
    frames, tokens, _ = q_in.shape
    frames_dev, rows = frames // 2, tokens // 2
    me, core = lax.axis_index("frm"), lax.axis_index("pos")
    half, side = me // 2, lax.rem(me, 2)
    head = 4 * slot + 2 * side + core
    window, stride = windows[head], strides[head]
    columns = head_columns(slot, side, core)
    mine = pl.ds(side * frames_dev, frames_dev)
    others = pl.ds((1 - side) * frames_dev, frames_dev)
    near, far = pl.ds(0, rows), pl.ds(rows, rows)

    copies = []
    for at, target in enumerate((q_in, k_in, v_in)):
        copies += [
            pltpu.make_async_copy(sources[at].at[:, :, columns], target.at[mine, near], load_sem.at[at, 0]),
            pltpu.make_async_copy(
                swapped.at[slot, side, at], target.at[mine, far], load_sem.at[at, 1]
            ),
            pltpu.make_async_copy(beside.at[at], target.at[others], load_sem.at[at, 2]),
        ]
    for kind, target in enumerate((kx_in, vx_in)):
        for at in range(2):
            copies.append(
                pltpu.make_async_copy(
                    keys[at].at[kind], target.at[pl.ds(at, 1)], far_sem.at[0, kind, at]
                )
            )
    for copy in copies:
        copy.start()
    inner = (me > 0) & (me < parts - 1)

    def halo_copies(source):
        return [
            pltpu.make_async_copy(
                halos[source].at[kind], target.at[pl.ds(2, WMAX)], far_sem.at[1, kind, 0]
            )
            for kind, target in enumerate((kx_in, vx_in))
        ]

    for taken, first in ((inner, 1), (jnp.logical_not(inner), 0)):

        @pl.when(taken)
        def _(first=first):
            for copy in halo_copies(first):
                copy.start()
            for copy in halo_copies(first):
                copy.wait()

    for copy in copies:
        copy.wait()

    score_scale = DH ** (-0.5) * math.log2(math.e)

    def place(keys_f32, values_f32, to_keys, to_values, block):
        at = pl.ds(pl.multiple_of(block * tokens, tokens), tokens)
        k_high, k_low = split(keys_f32)
        to_keys[at, 0:DH] = k_high
        to_keys[at, DH : 2 * DH] = k_high
        to_keys[at, 2 * DH : 3 * DH] = k_low
        v_high, v_low = split(values_f32.T)
        to_values[0:DH, at] = v_high
        to_values[DH : 2 * DH, at] = v_low

    def prepare(frame, carry):
        at = pl.ds(pl.multiple_of(frame * tokens, tokens), tokens)
        high, low = split(q_in[frame] * score_scale)
        q_cat[at, 0:DH] = high
        q_cat[at, DH : 2 * DH] = low
        q_cat[at, 2 * DH : 3 * DH] = high
        place(k_in[frame], v_in[frame], k_cat, v_cat, frame + WMAX)
        return carry

    lax.fori_loop(0, frames, prepare, 0)
    edge = jnp.where(half == 0, frames + WMAX, 0)
    edge_from = (jnp.where(half == 0, side, 2), jnp.where(half == 0, 2, 3))
    for at in range(WMAX):
        place(kx_in[edge_from[at]], vx_in[edge_from[at]], k_cat, v_cat, edge + at)
    key_frame = [frames * half, frames * half + frames_dev]
    for at in range(2):
        source, target = pl.ds((WMAX + at * frames_dev) * tokens, tokens), pl.ds(at * tokens, tokens)
        kg_cat[target, :] = k_cat[source, :]
        vg_cat[:, target] = v_cat[:, source]
        place(kx_in[at], vx_in[at], kg_cat, vg_cat, 2 + at)
        key_frame.append(lax.bitwise_xor(me, 2 + at) * frames_dev)
    global_bias = [jnp.where(lax.rem(frame, stride) == 0, 0.0, MASKED) for frame in key_frame]

    group = HALF_GROUP
    reach = 2 * WMAX + group
    group_rows = group * tokens
    lane_frame = lax.broadcasted_iota(jnp.int32, (1, group_rows), 1) // tokens
    lowest = WMAX * (1 - half)

    def per_group(step, carry):
        first = step * group + WMAX
        start = jnp.clip(first - WMAX, lowest, lowest + frames + WMAX - reach)
        q_part = q_cat[pl.ds(pl.multiple_of(step * group_rows, group_rows), group_rows), :]
        k_at = pl.ds(pl.multiple_of(start * tokens, tokens), reach * tokens)
        local_bias = [
            jnp.where(jnp.abs(start + at - first - lane_frame) <= window, 0.0, MASKED)
            for at in range(reach)
        ]
        local_part = attention(k_cat[k_at, :], local_bias, v_cat[:, k_at], q_part)
        global_part = attention(kg_cat[...], global_bias, vg_cat[...], q_part)
        difference = (global_part - local_part).T
        local_part = local_part.T
        for at in range(group):
            local[step * group + at] = local_part[at * tokens : (at + 1) * tokens]
            diff[step * group + at] = difference[at * tokens : (at + 1) * tokens]
        return carry

    lax.fori_loop(0, frames // group, per_group, 0)
    to_local = pltpu.make_async_copy(local, local_out, store_sem.at[0])
    to_local.start()
    table = waves(2 * frames, top)

    def gather(row, carry):
        at = pl.ds(pl.multiple_of(row * BLEND, BLEND), BLEND)
        parts_of = [diff[frame, at] for frame in range(frames)]
        for wave, values in enumerate(table):
            total = sum(value * part for value, part in zip(values, parts_of))
            sums[wave, at] = total * half_sign(wave, half)
        return carry

    lax.fori_loop(0, tokens // BLEND, gather, 0)
    to_sums = pltpu.make_async_copy(sums, sums_out, store_sem.at[1])
    to_sums.start()
    to_local.wait()
    to_sums.wait()


def attend_half(slot, parts, top, scalars, sources, swapped, beside, keys, halos):
    frames_dev, rows, _ = sources[0].shape
    frames, tokens = 2 * frames_dev, 2 * rows
    waves_count = 2 * top + 1
    f32, bf16 = jnp.float32, jnp.bfloat16
    return pl.pallas_call(
        functools.partial(attend_half_kernel, slot, parts, top),
        out_shape=[
            jax.ShapeDtypeStruct((frames, tokens, DH), f32),
            jax.ShapeDtypeStruct((waves_count, tokens, DH), f32),
        ],
        in_specs=[pl.BlockSpec(memory_space=pltpu.SMEM)] * 2
        + [pl.BlockSpec(memory_space=pl.ANY)] * 9,
        out_specs=[pl.BlockSpec(memory_space=pl.ANY)] * 2,
        scratch_shapes=[pltpu.VMEM((frames, tokens, DH), f32)] * 3
        + [pltpu.VMEM((4, tokens, DH), f32)] * 2
        + [
            pltpu.VMEM((frames * tokens, 3 * DH), bf16),
            pltpu.VMEM(((frames + 2 * WMAX) * tokens, 3 * DH), bf16),
            pltpu.VMEM((2 * DH, (frames + 2 * WMAX) * tokens), bf16),
            pltpu.VMEM((4 * tokens, 3 * DH), bf16),
            pltpu.VMEM((2 * DH, 4 * tokens), bf16),
            pltpu.VMEM((frames, tokens, DH), f32),
            pltpu.VMEM((frames, tokens, DH), f32),
            pltpu.VMEM((waves_count, tokens, DH), f32),
            pltpu.SemaphoreType.DMA((3, 3)),
            pltpu.SemaphoreType.DMA((2, 2, 2)),
            pltpu.SemaphoreType.DMA((2,)),
        ],
        cost_estimate=pl.CostEstimate(
            flops=12 * frames * tokens * 10 * tokens * DH,
            bytes_accessed=6 * frames * tokens * DH * 4,
            transcendentals=frames * tokens * 10 * tokens,
        ),
        compiler_params=pltpu.CompilerParams(vmem_limit_bytes=ATTEND_VMEM),
    )(*scalars[:2], *sources, swapped, beside, *keys, *halos)


def mix_kernel(first, slots, top, *refs):
    cutoffs, refs = refs[0], refs[1:]
    outs, scratch = refs[3 * slots : 3 * slots + 4], refs[3 * slots + 4 :]
    local, own, other, load_sem, store_sem = scratch
    _, frames, tokens, _ = local.shape
    frames_dev, rows = frames // 2, tokens // 2
    me, core = lax.axis_index("frm"), lax.axis_index("pos")
    half, side = me // 2, lax.rem(me, 2)
    copies = [
        [
            pltpu.make_async_copy(refs[slots * at + slot], target.at[slot], load_sem.at[slot, at])
            for at, target in enumerate((own, other, local))
        ]
        for slot in range(slots)
    ]
    for copy in sum(copies, []):
        copy.start()
    table = waves(2 * frames, top)
    mine = pl.ds(side * frames_dev, frames_dev)
    others = pl.ds((1 - side) * frames_dev, frames_dev)
    near, far = pl.ds(0, rows), pl.ds(rows, rows)
    stores = []
    for slot in range(slots):
        cutoff = cutoffs[4 * (first + slot) + 2 * side + core]
        scales = []
        for wave in range(len(table)):
            k = (wave + 1) // 2
            share = (1.0 if k == 0 else 2.0) / (2 * frames)
            scales.append(jnp.where(cutoff >= k, share, 0.0) * half_sign(wave, half))
        for copy in copies[slot]:
            copy.wait()

        def blend(row, carry, slot=slot, scales=scales):
            at = pl.ds(pl.multiple_of(row * BLEND, BLEND), BLEND)
            parts_of = [
                scale * (own[slot, wave, at] + other[slot, wave, at])
                for wave, scale in enumerate(scales)
            ]
            for frame in range(frames):
                local[slot, frame, at] += sum(
                    values[frame] * part for values, part in zip(table, parts_of)
                )
            return carry

        lax.fori_loop(0, tokens // BLEND, blend, 0)
        for at, span in enumerate(((others, near), (others, far), (mine, far), (mine, near))):
            stores.append(
                pltpu.make_async_copy(
                    local.at[slot, *span], outs[at], store_sem.at[slot, at]
                )
            )
            stores[-1].start()
    for copy in stores:
        copy.wait()


def mix(first, top, cutoffs, halves, passed):
    slots = len(halves)
    frames, tokens, _ = halves[0][0].shape
    sums = passed[0].shape
    piece = (frames // 2, tokens // 2, DH)
    return pl.pallas_call(
        functools.partial(mix_kernel, first, slots, top),
        out_shape=[jax.ShapeDtypeStruct(piece, jnp.float32)] * 4,
        in_specs=[pl.BlockSpec(memory_space=pltpu.SMEM)]
        + [pl.BlockSpec(memory_space=pl.ANY)] * (3 * slots),
        out_specs=[pl.BlockSpec(memory_space=pl.ANY)] * 4,
        scratch_shapes=[
            pltpu.VMEM((slots, frames, tokens, DH), jnp.float32),
            pltpu.VMEM((slots, *sums), jnp.float32),
            pltpu.VMEM((slots, *sums), jnp.float32),
            pltpu.SemaphoreType.DMA((slots, 3)),
            pltpu.SemaphoreType.DMA((slots, 4)),
        ],
        compiler_params=pltpu.CompilerParams(vmem_limit_bytes=MOVE_VMEM),
    )(cutoffs, *[x[1] for x in halves], *passed, *[x[0] for x in halves])


def across(value, hop, flip, chips=None):
    chips = range(lax.axis_size("frm")) if chips is None else chips
    pairs = [(2 * z + c, 2 * (z ^ hop) + (c ^ flip)) for z in chips for c in range(2)]
    return lax.ppermute(value, ("frm", "pos"), pairs)


def by_halves(queries, key_states, value_states, windows, strides, cutoffs):
    parts = lax.axis_size("frm")
    frames_dev, _, channels = queries.shape
    slots = channels // DH // 4 - 1
    frames = frames_dev * parts
    top = frames // 8
    table = jnp.asarray(lowpass_table(frames))
    scalars, sources = (windows, strides, cutoffs), (queries, key_states, value_states)
    inner = (parts // 2 - 1, parts // 2)
    packed = pack(4 * slots, parts, *sources, 1)
    packed, sources = lax.optimization_barrier((packed, sources))
    mine = [packed[0]] + [None] * (parts - 1)
    for hop in wires(parts):
        mine[hop] = around(packed[hop], hop)
    swapped = across(swap_pack(slots, *sources), 0, 1)
    beside, far_keys, far_halos = [], [], []
    for slot in range(slots):
        side, keys, halos = full_pack(slot, *sources, swapped)
        far_keys.append([])
        far_halos.append([])
        for at in range(2):
            far_halos[-1].append(across(halos[at], 2 + at, 0, inner))
            far_keys[-1].append(across(keys[at], 2 + at, 0))
        beside.append(across(side, 1, 0))
    theirs = []
    for hop in range(parts):
        theirs.append(swap(mine[hop]))
    done = attend_head(4 * slots, parts, scalars, table, mine, theirs, 1)
    landed = [done[0]] + [None] * (parts - 1)
    for hop in wires(parts):
        landed[hop] = around(done[hop], hop)
    pieces = []
    for slot in range(slots):
        half = attend_half(
            slot, parts, top, scalars, sources, swapped, beside[slot], far_keys[slot], far_halos[slot]
        )
        passed = across(half[1], 2, 0)
        mixed = mix(slot, top, cutoffs, [half], [passed])
        near = across(mixed[0], 1, 0)
        far = across(mixed[1], 1, 1)
        other = across(mixed[2], 0, 1)
        pieces.append([near, far, other, mixed[3]])
    return unpack(slots, parts, landed + sum(pieces, []), channels)


def around(value, hop):
    size = lax.axis_size("frm")
    return lax.ppermute(value, "frm", [(i, i ^ hop) for i in range(size)])


def swap(value):
    size = lax.axis_size("pos")
    return lax.ppermute(value, "pos", [(i, size - 1 - i) for i in range(size)])


def with_halo(value, sides, width):
    for axis, dim in sides:
        size, length = (lax.axis_size(axis), value.shape[dim])
        up = [(i, (i + 1) % size) for i in range(size - 1)]
        down = [(j, i) for i, j in up]
        last = lax.slice_in_dim(value, length - width, length, axis=dim)
        first = lax.slice_in_dim(value, 0, width, axis=dim)
        before = lax.ppermute(last, axis, up)
        after = lax.ppermute(first, axis, down)
        value = jnp.concatenate([before, value, after], axis=dim)
    return value


def attend(query_rows, key_rows, value_rows, allowed, score_scale):
    scores = (
        jnp.einsum("qhd,khd->hqk", query_rows, key_rows, precision=lax.Precision.HIGHEST)
        * score_scale
    )
    highest = jnp.max(jnp.where(allowed, scores, -1e30), axis=2, keepdims=True)
    weights = jnp.where(allowed, jnp.exp(scores - highest), 0.0)
    row_total = jnp.sum(weights, axis=2, keepdims=True)
    return jnp.einsum(
        "hqk,khd->qhd", weights / row_total, value_rows, precision=lax.Precision.HIGHEST
    )


def by_frames(queries, key_states, value_states, windows, strides, cutoffs):
    frames_dev, half_tokens, channels = queries.shape
    heads_local = channels // DH
    frame_groups = lax.axis_size("frm")
    pos_count = lax.axis_size("pos")
    total_frames = frames_dev * frame_groups
    halo_frames = frames_dev // 2
    score_scale = DH ** (-0.5)
    query_count = frames_dev * half_tokens
    query_rows = queries.reshape(query_count, heads_local, DH)
    query_blocks = queries.reshape(frames_dev, half_tokens, heads_local, DH)
    first_frame = lax.axis_index("frm") * frames_dev
    key_full, value_full = (
        lax.all_gather(key_states, "pos", axis=1, tiled=True),
        lax.all_gather(value_states, "pos", axis=1, tiled=True),
    )
    full_tokens = key_full.shape[1]
    stacked = jnp.stack([key_full, value_full])
    padded = with_halo(stacked, (("frm", 1),), halo_frames)
    window_span = 2 * halo_frames + 1
    span_rows = window_span * full_tokens
    span_offsets = jnp.arange(span_rows, dtype=jnp.int32) // full_tokens - halo_frames

    def local_frame(frame_local):
        query_part = lax.dynamic_index_in_dim(query_blocks, frame_local, 0, keepdims=False)
        block = lax.dynamic_slice_in_dim(padded, frame_local, window_span, 1)
        near_keys = block[0].reshape(span_rows, heads_local, DH)
        near_values = block[1].reshape(span_rows, heads_local, DH)
        near_frames = first_frame + frame_local + span_offsets
        inside = (near_frames >= 0) & (near_frames < total_frames)
        allowed = inside[None, None, :] & (
            jnp.abs(span_offsets)[None, None, :] <= windows[:, None, None]
        )
        return attend(query_part, near_keys, near_values, allowed, score_scale)

    local_out = lax.map(local_frame, jnp.arange(frames_dev, dtype=jnp.int32)).reshape(
        query_count, heads_local, DH
    )
    frame_keys = key_states[::KSTRIDE].reshape(-1, heads_local, DH)
    frame_values = value_states[::KSTRIDE].reshape(-1, heads_local, DH)
    rows_dev = frame_keys.shape[0]
    key_part = lax.all_gather(frame_keys, ("frm", "pos"), axis=0, tiled=True)
    value_part = lax.all_gather(frame_values, ("frm", "pos"), axis=0, tiled=True)
    row_count = key_part.shape[0]
    row_ids = jnp.arange(row_count, dtype=jnp.int32)
    frame_ids = (
        row_ids // rows_dev // pos_count * frames_dev + row_ids % rows_dev // half_tokens * KSTRIDE
    )
    allowed = (frame_ids[None, :] % strides[:, None] == 0)[:, None, :]
    scores = (
        jnp.einsum("qhd,khd->hqk", query_rows, key_part, precision=lax.Precision.HIGHEST)
        * score_scale
    )
    top_old = jnp.full((heads_local, query_count), -1e30, jnp.float32)
    top_new = jnp.maximum(top_old, jnp.max(jnp.where(allowed, scores, -1e30), axis=2))
    weights = jnp.where(allowed, jnp.exp(scores - top_new[:, :, None]), 0.0)
    total_new = jnp.sum(weights, axis=2)
    accum_new = jnp.einsum("hqk,khd->hqd", weights, value_part, precision=lax.Precision.HIGHEST)
    final_state = (top_new, total_new, accum_new)
    _, total_final, accum_final = final_state
    global_out = jnp.transpose(accum_final / total_final[:, :, None], (1, 0, 2))
    frequency = jnp.arange(total_frames, dtype=jnp.int32)
    phase_index = frequency[:, None] * frequency[None, :] % total_frames
    phases = 2.0 * math.pi / total_frames * phase_index.astype(jnp.float32)
    cos_table = jnp.cos(phases)
    sin_table = jnp.sin(phases)
    distance_freq = jnp.minimum(frequency, total_frames - frequency)
    low_keep = (distance_freq[None, :] <= cutoffs[:, None]).astype(jnp.float32)
    lowpass = (
        jnp.einsum("kf,hk,kg->hfg", cos_table, low_keep, cos_table, precision=lax.Precision.HIGHEST)
        + jnp.einsum(
            "kf,hk,kg->hfg", sin_table, low_keep, sin_table, precision=lax.Precision.HIGHEST
        )
    ) / total_frames
    group_items = half_tokens // frame_groups
    local_grid = local_out.reshape(frames_dev, frame_groups, group_items, channels)
    global_grid = global_out.reshape(frames_dev, frame_groups, group_items, channels)
    frame_block = lax.all_to_all(
        global_grid - local_grid, "frm", split_axis=1, concat_axis=0, tiled=True
    )
    frames_all = frame_block.shape[0]
    item_count = frame_block.shape[2]
    shaped = frame_block.reshape(frames_all, item_count, heads_local, DH)
    filtered_block = jnp.einsum(
        "hfg,gihd->fihd", lowpass, shaped, precision=lax.Precision.HIGHEST
    ).reshape(frame_block.shape)
    filtered = lax.all_to_all(filtered_block, "frm", split_axis=0, concat_axis=1, tiled=True)
    blended = local_grid + filtered
    return blended.reshape(frames_dev, half_tokens, channels)


def in_halves(heads_local, frames_dev, parts, pos_count):
    return heads_local % 4 == 0 and heads_local > 4 and frames_dev == KSTRIDE and (parts, pos_count) == (4, 2)


def shards(queries, key_states, value_states, windows, strides, cutoffs):
    heads_local = queries.shape[2] // DH
    if in_halves(heads_local, queries.shape[0], lax.axis_size("frm"), lax.axis_size("pos")):
        return by_halves(queries, key_states, value_states, windows, strides, cutoffs)
    return by_frames(queries, key_states, value_states, windows, strides, cutoffs)


def solution(mesh):
    in_specs = (
        P(("grp", "frm"), "pos", "head"),
        P(("grp", "frm"), "pos", "head"),
        P(("grp", "frm"), "pos", "head"),
        P("head"),
        P("head"),
        P("head"),
    )
    out_specs = P(("grp", "frm"), "pos", "head")
    return jax.shard_map(
        shards, mesh=mesh, in_specs=in_specs, out_specs=out_specs, check_vma=False
    )
```
